128 devices in a mesh: group: 16 (over y, x), tensor: 8 (over z, core).
Axes of the slice: x: 4, y: 4, z: 4, core: 2. Of those that a mesh axis runs over, the one named last changes fastest.
Arguments:
- left_table: bfloat16 [1024, 8, 8192], P('group', 'tensor'), may hold values from -6 to 6
- right_table: bfloat16 [1024, 8, 8192], P('group', 'tensor'), may hold values from -6 to 6
- left_owner: int32 [256, 1], P('group'), may hold values from 0 to 15; in each aligned block of 16 rows (0 to 15, 16 to 31, ...) at most 2 rows name the same one
- left_row: int32 [256], P('group'), may hold values from 0 to 63
- right_owner: int32 [256, 1], P('group'), may hold values from 0 to 15; in each aligned block of 16 rows (0 to 15, 16 to 31, ...) at most 2 rows name the same one
- right_row: int32 [256], P('group'), may hold values from 0 to 63
- pair_count: int32 [16], P('group'), may hold values from 1 to 16, 128 in all
- norm_gain: float32 [8192], replicated, may hold values from 0.1 to 1.9
- query_weight: bfloat16 [8192, 4096], P(None, 'tensor'), may hold values from -0.0625 to 0.0625
- key_weight: bfloat16 [8192, 1024], P(None, 'tensor'), may hold values from -0.0625 to 0.0625
- value_weight: bfloat16 [8192, 1024], P(None, 'tensor'), may hold values from -0.0625 to 0.0625
- output_weight: bfloat16 [4096, 8192], P('tensor'), may hold values from -0.09375 to 0.09375
Outputs:
- left_sums: float32 [1024, 8192], P('group', 'tensor')
- right_sums: float32 [1024, 8192], P('group', 'tensor')
The draws below stay inside these ranges and needn't reach their ends.
Inputs may be any that keep to these rules, and one draw needn't show every extreme that they name: `left_owner`: among the 16 pair slots of one group, at most 2 have the same left owner; some owner is named by exactly 2 of them in some groups. `right_owner`: among the 16 pair slots of one group, at most 2 have the same right owner; some owner is named by exactly 2 of them in some groups. `pair_count`: the counts sum to 128 and one group has all 16 slots live.
All inputs are finite; a program needn't handle non-finite values.
Results may differ from the reference program's by a relative error of at most 0.0035.
Values may be sent and summed in bfloat16 or wider, within the bound.
A program may use at most 128 MiB of HBM per device.

```python
import math
import jax
import jax.numpy as jnp
import numpy as np
from jax import lax

D = 8192
HEADS = 32
KV_HEADS = 8
HEAD_DIM = 128
REC_TOKENS = 8
ROWS_DEV = 64
PAIRS_DEV = 16
PAIR_CAP = 2
TABLE_ROWS = 1024
PAIRS = 256
N_GROUP = 16


def set_ends(entries, stream_key, least, largest):
    extent = entries.shape
    place = [jax.random.randint(jax.random.fold_in(stream_key, axis), (), 0, extent[axis]) for axis in range(len(extent))]
    entries = entries.at[tuple(place)].set(least)
    longest = extent.index(max(extent))
    place[longest] = (place[longest] + 1) % extent[longest]
    return entries.at[tuple(place)].set(largest)


def steps_of(own_key, dims, split, smallest, largest):
    factor_of = 1.0
    for axis_at, blocks in split:
        steps = jax.random.uniform(jax.random.fold_in(jax.random.fold_in(own_key, 6), axis_at), (blocks,), jnp.float32, smallest / len(split), largest / len(split))
        factor_of = factor_of * jnp.repeat(jnp.exp(steps), dims[axis_at] // blocks).reshape((-1,) + (1,) * (len(dims) - 1 - axis_at))
    return factor_of


def length_profile(count, total, most, skew):
    loads = [(1 << 20) // math.isqrt(rank ** skew) + 1 for rank in range(2, count + 1)]
    surplus, given = total - most - (count - 1), [1] * (count - 1)
    while surplus > 0:
        candidates = [i for i in range(count - 1) if given[i] < most]
        pool, budget = sum([loads[i] for i in candidates]), surplus
        for i in candidates:
            more = min(most - given[i], max(1, budget * loads[i] // pool), surplus)
            given[i] = given[i] + more
            surplus = surplus - more
    return np.array([most] + given)


def ragged(own_key, number_of, total, bound, slope):
    if number_of == 2:
        one = jax.random.randint(own_key, (), max(1, total - bound), min(bound, total - 1) + 1)
        return jnp.stack([one, total - one])
    lengths = jnp.asarray(length_profile(number_of, total, bound, slope), jnp.int32)
    pairs = (number_of - 1) // 2
    donor, receiver = lengths[1:1 + 2 * pairs:2], lengths[2:2 + 2 * pairs:2]
    margin = jnp.minimum(donor - 1, bound - receiver)
    moved = jax.random.randint(jax.random.fold_in(own_key, 1), (pairs,), 0, 1 << 20) % (margin + 1)
    lengths = lengths.at[1:1 + 2 * pairs:2].set(donor - moved).at[2:2 + 2 * pairs:2].set(receiver + moved)
    return lengths[jax.random.permutation(jax.random.fold_in(own_key, 2), number_of)]


def deal_out(rng, own, number, rows, amount, top, reach, slope):
    order = jax.random.permutation(rng, amount)
    crowded, common = load_shares(amount, rows * top, reach, slope, True), load_shares(amount, rows * top, reach, slope, False)
    places = jnp.arange(amount)

    def named(sizes, rotation):
        used = int((sizes > 0).sum())
        fixed = max(1, used // 4)
        passed = fixed + (places - fixed + rotation * (used - fixed)) % max(1, amount - fixed)
        return jnp.zeros((amount,), jnp.int32).at[order[jnp.where(places < fixed, places, passed)]].set(jnp.asarray(sizes, jnp.int32))

    sizes = jnp.where(number % 4 == 0, named(crowded, number // 4), named(common, number - number // 4 - 1))
    mixed = jax.random.permutation(jax.random.fold_in(own, 3), amount)
    donor, taker = mixed[0:amount // 2 * 2:2], mixed[1:amount // 2 * 2:2]
    slack = jnp.minimum(sizes[donor] - 1, reach - sizes[taker]) // 2
    slack = jnp.where((donor == order[0]) | (taker == order[0]) | (sizes[taker] == 0), 0, jnp.maximum(slack, 0))
    passed = jax.random.randint(jax.random.fold_in(own, 4), (amount // 2,), 0, 1 << 20) % (slack + 1)
    sizes = sizes.at[donor].add(-passed).at[taker].add(passed)
    labels = jnp.searchsorted(jnp.cumsum(sizes), jnp.arange(rows * top), side="right").astype(jnp.int32)
    table = labels.reshape(top, rows).T
    table = table[jax.random.permutation(jax.random.fold_in(own, 1), rows)]
    rotation = jax.random.randint(jax.random.fold_in(own, 2), (rows, 1), 0, top)
    return jnp.take_along_axis(table, (jnp.arange(top)[None, :] + rotation) % top, axis=1)


def load_shares(number_of, total, bound, skew, full):
    weights = [(1 << 20) // math.isqrt(grade ** skew) + 1 for grade in range(1, number_of + 1)]
    largest = bound if full else min(bound, max(-(-total // number_of), total * weights[0] // sum(weights)))
    least = 1 if total - largest >= number_of - 1 else 0
    given, rest = [largest] + [least] * (number_of - 1), total - largest - least * (number_of - 1)
    while rest > 0:
        movable = [i for i in range(1, number_of) if given[i] < largest] or [i for i in range(1, number_of) if given[i] < bound]
        pool, remaining = sum([weights[i] for i in movable]), rest
        for i in movable:
            more = min(bound - given[i], max(1, remaining * weights[i] // pool), rest)
            given[i] = given[i] + more
            rest = rest - more
    return np.array(given)


def centred(stream_key, extent, scale, bound, split=(), kind=jnp.bfloat16):
    array = jax.random.normal(stream_key, extent, jnp.float32) * scale
    if len(split) > 0:
        array = steps_of(stream_key, extent, split, -0.22, 0.18) * array
    return jnp.clip(array, min=-bound, max=bound).astype(kind)


def setup_inputs(seed: int = 0) -> dict:
    key_of = jax.random.split(jax.random.key(seed), 13)
    left_table = centred(key_of[0], (TABLE_ROWS, REC_TOKENS, D), 1.0, 6.0, ((0, 16), (1, 8)))
    right_table = centred(key_of[1], (TABLE_ROWS, REC_TOKENS, D), 1.0, 6.0, ((0, 16), (1, 8)))
    left_owner_keys = jax.random.split(jax.random.fold_in(key_of[2], 1), PAIRS // PAIRS_DEV)
    left_owner_turns = jax.random.permutation(jax.random.fold_in(key_of[2], 3), PAIRS // PAIRS_DEV)
    left_owner = jax.vmap(lambda own, number: deal_out(jax.random.fold_in(key_of[2], 2), own, number, PAIRS_DEV, N_GROUP, 1, PAIR_CAP, 2))(left_owner_keys, left_owner_turns).reshape((PAIRS, 1))
    left_row = set_ends(jax.random.randint(key_of[3], (PAIRS,), 0, ROWS_DEV), jax.random.fold_in(key_of[3], 1), 0, ROWS_DEV - 1).astype(jnp.int32)
    right_owner_keys = jax.random.split(jax.random.fold_in(key_of[4], 1), PAIRS // PAIRS_DEV)
    right_owner_turns = jax.random.permutation(jax.random.fold_in(key_of[4], 3), PAIRS // PAIRS_DEV)
    right_owner = jax.vmap(lambda own, number: deal_out(jax.random.fold_in(key_of[4], 2), own, number, PAIRS_DEV, N_GROUP, 1, PAIR_CAP, 2))(right_owner_keys, right_owner_turns).reshape((PAIRS, 1))
    right_row = set_ends(jax.random.randint(key_of[5], (PAIRS,), 0, ROWS_DEV), jax.random.fold_in(key_of[5], 1), 0, ROWS_DEV - 1).astype(jnp.int32)
    pair_count = ragged(key_of[6], N_GROUP, N_GROUP * PAIRS_DEV // 2, PAIRS_DEV, 2).astype(jnp.int32)
    norm_gain = jnp.clip(1.0 + 0.18 * jax.random.normal(key_of[7], (D,), jnp.float32), 0.1, 1.9)
    query_weight = centred(key_of[8], (D, HEADS * HEAD_DIM), D ** -0.5, 0.0625, ((1, 8),))
    key_weight = centred(key_of[9], (D, KV_HEADS * HEAD_DIM), D ** -0.5, 0.0625, ((1, 8),))
    value_weight = centred(key_of[10], (D, KV_HEADS * HEAD_DIM), D ** -0.5, 0.0625, ((1, 8),))
    output_weight = centred(key_of[11], (HEADS * HEAD_DIM, D), (HEADS * HEAD_DIM) ** -0.5, 0.09375, ((0, 8),))
    return dict(left_table=left_table, right_table=right_table, left_owner=left_owner, left_row=left_row, right_owner=right_owner, right_row=right_row, pair_count=pair_count, norm_gain=norm_gain, query_weight=query_weight, key_weight=key_weight, value_weight=value_weight, output_weight=output_weight)


score_scale = 4.0

def pair_states(left_tokens, right_tokens, norm_gain, query_weight, key_weight, value_weight, output_weight):
    inputs = jnp.concatenate([left_tokens, right_tokens], axis=1)
    count = inputs.shape[0]
    length = inputs.shape[1]
    flat = inputs.reshape(count * length, D).astype(jnp.float32)
    scale = lax.rsqrt(lax.optimization_barrier(jnp.mean(flat * flat, axis=-1, keepdims=True)) + 1e-05)
    normed = (flat * scale * norm_gain[None, :]).astype(jnp.bfloat16)
    q_raw = jnp.dot(normed, query_weight, preferred_element_type=jnp.float32)
    k_raw = jnp.dot(normed, key_weight, preferred_element_type=jnp.float32)
    values = jnp.dot(normed, value_weight, preferred_element_type=jnp.float32).astype(jnp.bfloat16)
    q_heads = q_raw.reshape(count * length, HEADS, HEAD_DIM)
    k_heads = k_raw.reshape(count * length, KV_HEADS, HEAD_DIM)
    q_norm = (q_heads * lax.rsqrt(lax.optimization_barrier(jnp.mean(q_heads * q_heads, axis=-1, keepdims=True)) + 1e-06)).astype(jnp.bfloat16)
    k_norm = (k_heads * lax.rsqrt(lax.optimization_barrier(jnp.mean(k_heads * k_heads, axis=-1, keepdims=True)) + 1e-06)).astype(jnp.bfloat16)
    share = HEADS // KV_HEADS
    q_five = q_norm.reshape(count, length, KV_HEADS, share, HEAD_DIM).astype(jnp.float32)
    k_four = k_norm.reshape(count, length, KV_HEADS, HEAD_DIM).astype(jnp.float32)
    v_four = values.reshape(count, length, KV_HEADS, HEAD_DIM).astype(jnp.float32)
    scores = jnp.einsum('pqkgd,pskd->pkgqs', q_five, k_four) * (score_scale / HEAD_DIM)
    expo = jnp.exp(scores)
    weights = (expo / lax.optimization_barrier(jnp.sum(expo, axis=-1, keepdims=True))).astype(jnp.bfloat16)
    context = jnp.einsum('pkgqs,pskd->pqkgd', weights.astype(jnp.float32), v_four).astype(jnp.bfloat16)
    context = context.reshape(count * length, HEADS * HEAD_DIM)
    attended = jnp.dot(context, output_weight, preferred_element_type=jnp.float32)
    total = flat + attended
    return lax.optimization_barrier(jnp.mean(total.reshape(count, length, D), axis=1))

def reference(left_table, right_table, left_owner, left_row, right_owner, right_row, pair_count, norm_gain, query_weight, key_weight, value_weight, output_weight):
    left_ids = (left_owner[:, 0] * ROWS_DEV + left_row).astype(jnp.int32)
    right_ids = (right_owner[:, 0] * ROWS_DEV + right_row).astype(jnp.int32)

    def one_group(ids):
        return pair_states(left_table[ids[0]], right_table[ids[1]], norm_gain, query_weight, key_weight, value_weight, output_weight)
    pooled = lax.map(one_group, (left_ids.reshape(N_GROUP, PAIRS_DEV), right_ids.reshape(N_GROUP, PAIRS_DEV)))
    pooled = pooled.reshape(N_GROUP * PAIRS_DEV, D)
    live = (jnp.arange(PAIRS_DEV, dtype=jnp.int32)[None, :] < pair_count[:, None]).reshape(N_GROUP * PAIRS_DEV)
    pooled = jnp.where(live[:, None], pooled, jnp.zeros_like(pooled))
    left_sums = jax.ops.segment_sum(pooled, left_ids, num_segments=ROWS_DEV * N_GROUP)
    right_sums = jax.ops.segment_sum(pooled, right_ids, num_segments=ROWS_DEV * N_GROUP)
    return (left_sums, right_sums)
```

```python
import functools

import jax
import jax.numpy as jnp
from jax import lax
from jax.experimental import pallas as pl
from jax.experimental.pallas import tpu as pltpu
from jax.sharding import PartitionSpec as P

HEAD_DIM = 128
SCORE_SCALE = 4.0
MESH = pl.DeviceIdType.MESH
GROUPS = 16
SIDE = 4
TENSORS = 8
PAIRS = 16
SLOTS = GROUPS * 8
ROWS = 64
F32 = jnp.float32
BF16 = jnp.bfloat16


def iota(shape, axis):
    return lax.broadcasted_iota(jnp.int32, shape, axis)


def group_shift(g, k, sign):
    y, x = g // SIDE, g % SIDE
    ky, kx = k // SIDE, k % SIDE
    return ((y + sign * ky + SIDE) % SIDE) * SIDE + (x + sign * kx + SIDE) % SIDE


def pieces(value):
    high = value.astype(BF16)
    rest = value - high.astype(F32)
    middle = rest.astype(BF16)
    low = (rest - middle.astype(F32)).astype(BF16)
    return high, middle, low


def to_column(row):
    eye = iota((PAIRS, PAIRS), 0) == iota((PAIRS, PAIRS), 1)
    return jnp.sum(jnp.where(eye, row, 0.0), axis=1, keepdims=True)


def slot_keys(owner_row, me):
    owner_col = to_column(owner_row)
    first = iota((PAIRS, PAIRS), 0)
    second = iota((PAIRS, PAIRS), 1)
    same = owner_col == owner_row
    rank_row = jnp.sum(jnp.where(same & (first < second), 1.0, 0.0), axis=0, keepdims=True)
    rank_col = jnp.sum(jnp.where(same & (second < first), 1.0, 0.0), axis=1, keepdims=True)
    want_row = owner_row * 2.0 + rank_row

    def place(owner, rank):
        whole = owner.astype(jnp.int32)
        y, x = me // SIDE, me % SIDE
        ky = (y - whole // SIDE + SIDE) % SIDE
        kx = (x - whole % SIDE + SIDE) % SIDE
        return ((ky * SIDE + kx) * 2).astype(F32) + rank

    return want_row, place(owner_row, rank_row), place(owner_col, rank_col)


def requests(want_row, row_row, me):
    sub = iota((SLOTS, PAIRS), 0)
    k = sub // 8
    y, x = me // SIDE, me % SIDE
    owner = ((y - k // SIDE + SIDE) % SIDE) * SIDE + (x - k % SIDE + SIDE) % SIDE
    want = (owner * 2 + sub % 2).astype(F32)
    found = jnp.sum(jnp.where(want_row == want, row_row + 1.0, 0.0), axis=1, keepdims=True) - 1.0
    return jnp.broadcast_to(found, (SLOTS, 128))


def pick_matrix(wanted):
    both = jnp.concatenate([wanted, wanted], axis=1)
    lane = iota((SLOTS, 4 * ROWS), 1)
    quarter = (iota((SLOTS, 4 * ROWS), 0) % 8) // 2
    hit = (both == (lane % ROWS).astype(F32)) & (lane // ROWS == quarter)
    return jnp.where(hit, 1.0, 0.0).astype(BF16)


def pack_matrix(place_col):
    tall = jnp.concatenate([place_col] * 4, axis=0)
    lane = iota((4 * PAIRS, SLOTS), 1)
    quarter = iota((4 * PAIRS, SLOTS), 0) // PAIRS
    key = ((lane // 8) * 2 + lane % 2).astype(F32)
    hit = (tall == key) & ((lane % 8) // 2 == quarter)
    return jnp.where(hit, 1.0, 0.0).astype(BF16)


def spread_matrix(place_row):
    wide = jnp.concatenate([place_row] * 4, axis=1)
    sub = iota((SLOTS, 4 * PAIRS), 0)
    quarter = iota((SLOTS, 4 * PAIRS), 1) // PAIRS
    key = ((sub // 8) * 2 + sub % 2).astype(F32)
    hit = (wide == key) & ((sub % 8) // 2 == quarter)
    return jnp.where(hit, 1.0, 0.0).astype(BF16)


def dot(a, b):
    return jnp.dot(a, b, preferred_element_type=F32)


def kernel(
    lo_ref, lr_ref, ro_ref, rr_ref, count_ref, gain_ref,
    lt_ref, rt_ref, wq_ref, wk_ref, wv_ref, wo_ref,
    lout_ref, rout_ref,
    table, qkv_w, out_w, outbox, inbox, picked, arrived, tokens, flat, resid,
    acc, part, parts_in, fin_out, fin_in,
    load_sem, idx_s, idx_r, row_s, row_r, ag_s, ag_r, rs_s, rs_r, fin_s, fin_r,
):
    g = lax.axis_index("group")
    t = lax.axis_index("tensor")
    z, c = t // 2, t % 2
    width = out_w.shape[1]
    quarter = width // 4
    share = width // TENSORS

    loads = []

    def load(src, dst):
        copy = pltpu.make_async_copy(src, dst, load_sem.at[len(loads)])
        copy.start()
        loads.append(copy)

    for side, ref in enumerate((lt_ref, rt_ref)):
        for q in range(4):
            load(ref.at[:, pl.ds(q * quarter, quarter)], table.at[side, pl.ds(q * ROWS, ROWS), :])

    barrier = pltpu.get_barrier_semaphore()
    for k in range(1, GROUPS):
        pl.semaphore_signal(
            barrier, inc=1, device_id=(group_shift(g, k, 1), t), device_id_type=MESH
        )
    for j in range(1, TENSORS):
        pl.semaphore_signal(
            barrier, inc=1, device_id=(g, (t + j) % TENSORS), device_id_type=MESH
        )

    q_cols = wq_ref.shape[1]
    kv_cols = wk_ref.shape[1]
    load(wq_ref, qkv_w.at[:, pl.ds(0, q_cols)])
    load(wk_ref, qkv_w.at[:, pl.ds(q_cols, kv_cols)])
    load(wv_ref, qkv_w.at[:, pl.ds(q_cols + kv_cols, kv_cols)])
    load(wo_ref, out_w)

    owners = (lo_ref[...].astype(F32), ro_ref[...].astype(F32))
    rows = (lr_ref[...].astype(F32), rr_ref[...].astype(F32))
    keys = [slot_keys(owners[side], g) for side in range(2)]
    for side in range(2):
        asked = requests(keys[side][0], rows[side], g)
        outbox[:, :, pl.ds(side * 128, 128)] = asked.reshape(GROUPS, 8, 128)

    pl.semaphore_wait(barrier, GROUPS - 1 + TENSORS - 1)

    idx = []
    for k in range(1, GROUPS):
        copy = pltpu.make_async_remote_copy(
            src_ref=outbox.at[k], dst_ref=inbox.at[k],
            send_sem=idx_s.at[k], recv_sem=idx_r.at[k],
            device_id=(group_shift(g, k, -1), t), device_id_type=MESH,
        )
        copy.start()
        idx.append(copy)
    inbox[0] = outbox[0]
    for copy in loads[:8]:
        copy.wait()
    for copy in idx:
        copy.wait_recv()

    chunk = 512
    picks = []
    row_copies = [[], []]
    for side in range(2):
        wanted = inbox[:, :, pl.ds(side * 128, 128)].reshape(SLOTS, 128)
        pick = pick_matrix(wanted)
        picks.append(pick)
        for n in range(quarter // chunk):
            cols = pl.ds(n * chunk, chunk)
            picked[side, :, :, cols] = (
                dot(pick, table[side, :, cols]).astype(BF16).reshape(GROUPS, 8, chunk)
            )
        for k in range(1, GROUPS):
            copy = pltpu.make_async_remote_copy(
                src_ref=picked.at[side, k], dst_ref=arrived.at[side, k],
                send_sem=row_s.at[side, k], recv_sem=row_r.at[side, k],
                device_id=(group_shift(g, k, 1), t), device_id_type=MESH,
            )
            copy.start()
            row_copies[side].append(copy)
        arrived[side, 0] = picked[side, 0]

    up = ((z + 1) % SIDE) * 2 + c
    down = ((z + SIDE - 1) % SIDE) * 2 + c
    far = ((z + 2) % SIDE) * 2 + c
    twin = z * 2 + 1 - c

    def send(side, number, block, half, target):
        place = tokens.at[side, block]
        if half is not None:
            place = place.at[pl.ds(half * 8, 8)]
        copy = pltpu.make_async_remote_copy(
            src_ref=place, dst_ref=place,
            send_sem=ag_s.at[side, number], recv_sem=ag_r.at[side, number],
            device_id=(g, target), device_id_type=MESH,
        )
        copy.start()
        return copy

    gathers = [{}, {}]
    for side in range(2):
        for copy in row_copies[side]:
            copy.wait_recv()
        pack = pack_matrix(keys[side][2])
        squares = jnp.zeros((PAIRS, 1), F32)
        for n in range(quarter // chunk):
            cols = pl.ds(n * chunk, chunk)
            got = dot(pack, arrived[side, :, :, cols].reshape(SLOTS, chunk))
            for q in range(4):
                one = got[q * PAIRS : (q + 1) * PAIRS]
                flat[:, pl.ds(q * quarter + n * chunk, chunk)] = one
                squares = squares + jnp.sum(one * one, axis=1, keepdims=True)
        scale = lax.rsqrt(squares / width + 1e-05)
        for n in range(width // chunk):
            cols = pl.ds(n * chunk, chunk)
            one = flat[:, cols]
            tokens[side, t, :, cols] = (one * scale * gain_ref[:, cols]).astype(BF16)
            if side == 0:
                resid[:, cols] = one
            else:
                resid[:, cols] = (resid[:, cols] + one) * (1.0 / 16.0)
        for number, target in ((0, up), (1, down), (2, twin)):
            gathers[side][number] = send(side, number, t, None, target)

    def forward_near(side):
        gathers[side][0].wait_recv()
        gathers[side][3] = send(side, 3, down, 0, up)
        gathers[side][4] = send(side, 4, down, None, twin)
        gathers[side][1].wait_recv()
        gathers[side][5] = send(side, 5, up, 1, down)
        gathers[side][6] = send(side, 6, up, None, twin)

    def forward_far(side):
        gathers[side][3].wait_recv()
        gathers[side][5].wait_recv()
        gathers[side][7] = send(side, 7, far, None, twin)

    def project(side):
        for number in (2, 4, 6, 7):
            gathers[side][number].wait_recv()
        depth = 512
        acc[side] = jnp.zeros_like(acc[side])

        @pl.loop(0, width // depth)
        def _(i):
            cols = pl.ds(pl.multiple_of(i * depth, depth), depth)
            a = tokens[side, :, :, cols].reshape(TENSORS * PAIRS, depth)
            acc[side] += dot(a, qkv_w[cols, :])

    forward_near(0)
    forward_far(0)
    forward_near(1)
    for copy in loads[8:11]:
        copy.wait()
    project(0)
    forward_far(1)
    project(1)

    count = 2 * TENSORS * PAIRS
    full = acc[...].reshape(count, q_cols + 2 * kv_cols)
    key = full[:, q_cols : q_cols + HEAD_DIM]
    value = full[:, q_cols + kv_cols : q_cols + kv_cols + HEAD_DIM].astype(BF16)

    def unit(rows_):
        return (
            rows_ * lax.rsqrt(jnp.mean(rows_ * rows_, axis=-1, keepdims=True) + 1e-06)
        ).astype(BF16)

    key = unit(key)
    mask = (iota((count, count), 0) % PAIRS) == (iota((count, count), 1) % PAIRS)
    pool = jnp.where(
        iota((PAIRS, count), 0) == iota((PAIRS, count), 1) % PAIRS, 1.0, 0.0
    ).astype(BF16)
    pooled = []
    for head in range(q_cols // HEAD_DIM):
        query = unit(full[:, head * HEAD_DIM : (head + 1) * HEAD_DIM])
        scores = lax.dot_general(
            query, key, (((1,), (1,)), ((), ())), preferred_element_type=F32
        ) * (SCORE_SCALE / HEAD_DIM)
        expo = jnp.where(mask, jnp.exp(scores), 0.0)
        weights = (expo / jnp.sum(expo, axis=-1, keepdims=True)).astype(BF16)
        context = dot(weights, value).astype(BF16)
        pooled.append(dot(pool, context) * (1.0 / 16.0))
    pooled = jnp.concatenate(pooled, axis=1)
    high = pooled.astype(BF16)
    low = (pooled - high.astype(F32)).astype(BF16)
    both = jnp.concatenate([high, low], axis=0)

    loads[11].wait()
    sums = []
    for j in (4, 5, 2, 3, 6, 7, 1, 0):
        target = ((z + j // 2) % SIDE) * 2 + (c + j % 2) % 2
        cols = pl.ds(pl.multiple_of(target * share, share), share)
        got = dot(both, out_w[:, cols])
        part[j] = got[:PAIRS] + got[PAIRS:] + resid[:, cols]
        if j > 0:
            copy = pltpu.make_async_remote_copy(
                src_ref=part.at[j], dst_ref=parts_in.at[j],
                send_sem=rs_s.at[j], recv_sem=rs_r.at[j],
                device_id=(g, target), device_id_type=MESH,
            )
            copy.start()
            sums.append(copy)
    for copy in sums:
        copy.wait_recv()
    total = part[0]
    for j in range(1, TENSORS):
        total = total + parts_in[j]
    live = iota((PAIRS, share), 0) < count_ref[...]
    total = jnp.where(live, total, 0.0)

    piece = share // 4
    stacked = jnp.concatenate([total[:, q * piece : (q + 1) * piece] for q in range(4)], axis=0)
    parts3 = pieces(stacked)
    for side in range(2):
        spread = spread_matrix(keys[side][1])
        got = dot(spread, parts3[0]) + dot(spread, parts3[1]) + dot(spread, parts3[2])
        fin_out[:, :, pl.ds(side * piece, piece)] = got.reshape(GROUPS, 8, piece)
    finals = []
    for k in range(1, GROUPS):
        copy = pltpu.make_async_remote_copy(
            src_ref=fin_out.at[k], dst_ref=fin_in.at[k],
            send_sem=fin_s.at[k], recv_sem=fin_r.at[k],
            device_id=(group_shift(g, k, -1), t), device_id_type=MESH,
        )
        copy.start()
        finals.append(copy)
    fin_in[0] = fin_out[0]
    for copy in finals:
        copy.wait_recv()
    for side, out in enumerate((lout_ref, rout_ref)):
        came = pieces(fin_in[:, :, pl.ds(side * piece, piece)].reshape(SLOTS, piece))
        got = jnp.zeros((4 * ROWS, piece), F32)
        for one in came:
            got = got + lax.dot_general(
                picks[side], one, (((0,), (0,)), ((), ())), preferred_element_type=F32
            )
        for q in range(4):
            out[:, pl.ds(q * piece, piece)] = got[q * ROWS : (q + 1) * ROWS]

    for copy in idx + row_copies[0] + row_copies[1] + sums + finals:
        copy.wait_send()
    for side in range(2):
        for copy in gathers[side].values():
            copy.wait_send()


def on_device(
    left_table, right_table, left_owner, left_row, right_owner, right_row, pair_count,
    norm_gain, query_weight, key_weight, value_weight, output_weight,
):
    width = left_table.shape[2]
    quarter = width // 4
    share = width // TENSORS
    qkv = query_weight.shape[1] + 2 * key_weight.shape[1]
    vmem = pl.BlockSpec(memory_space=pltpu.VMEM)
    hbm = pl.BlockSpec(memory_space=pl.ANY)
    dma = pltpu.SemaphoreType.DMA
    out = jax.ShapeDtypeStruct((ROWS, share), F32)
    return pl.pallas_call(
        kernel,
        out_shape=(out, out),
        in_specs=[vmem] * 6 + [hbm] * 6,
        out_specs=(vmem, vmem),
        scratch_shapes=[
            pltpu.VMEM((2, 4 * ROWS, quarter), BF16),
            pltpu.VMEM((width, qkv), BF16),
            pltpu.VMEM(output_weight.shape, BF16),
            pltpu.VMEM((GROUPS, 8, 256), F32),
            pltpu.VMEM((GROUPS, 8, 256), F32),
            pltpu.VMEM((2, GROUPS, 8, quarter), BF16),
            pltpu.VMEM((2, GROUPS, 8, quarter), BF16),
            pltpu.VMEM((2, TENSORS, PAIRS, width), BF16),
            pltpu.VMEM((PAIRS, width), F32),
            pltpu.VMEM((PAIRS, width), F32),
            pltpu.VMEM((2, TENSORS * PAIRS, qkv), F32),
            pltpu.VMEM((TENSORS, PAIRS, share), F32),
            pltpu.VMEM((TENSORS, PAIRS, share), F32),
            pltpu.VMEM((GROUPS, 8, share // 2), F32),
            pltpu.VMEM((GROUPS, 8, share // 2), F32),
            dma((12,)),
            dma((GROUPS,)), dma((GROUPS,)),
            dma((2, GROUPS)), dma((2, GROUPS)),
            dma((2, 8)), dma((2, 8)),
            dma((TENSORS,)), dma((TENSORS,)),
            dma((GROUPS,)), dma((GROUPS,)),
        ],
        compiler_params=pltpu.CompilerParams(
            collective_id=0, has_side_effects=True, vmem_limit_bytes=56 * 1024 * 1024
        ),
    )(
        left_owner.reshape(1, PAIRS), left_row.reshape(1, PAIRS),
        right_owner.reshape(1, PAIRS), right_row.reshape(1, PAIRS),
        pair_count.reshape(1, 1), norm_gain.reshape(1, width),
        left_table.reshape(ROWS, width), right_table.reshape(ROWS, width),
        query_weight, key_weight, value_weight, output_weight,
    )


def solution(mesh):
    return jax.shard_map(
        on_device,
        mesh=mesh,
        in_specs=(
            P("group", "tensor", None), P("group", "tensor", None),
            P("group", None), P("group"), P("group", None), P("group"), P("group"), P(),
            P(None, "tensor"), P(None, "tensor"), P(None, "tensor"), P("tensor", None),
        ),
        out_specs=(P("group", "tensor"), P("group", "tensor")),
        check_vma=False,
    )
```

```python
import jax
import jax.numpy as jnp
from jax import lax
from jax.experimental import pallas as pl
from jax.experimental.pallas import tpu as pltpu
from jax.sharding import PartitionSpec as P

HEAD_DIM = 128
SCORE_SCALE = 4.0
MESH = pl.DeviceIdType.MESH
GROUPS = 16
SIDE = 4
TENSORS = 8
PAIRS = 16
SLOTS = GROUPS * 8
ROWS = 64
CHUNKS = 4
F32 = jnp.float32
BF16 = jnp.bfloat16


def iota(shape, axis):
    return lax.broadcasted_iota(jnp.int32, shape, axis)


def group_shift(g, k, sign):
    y, x = g // SIDE, g % SIDE
    ky, kx = k // SIDE, k % SIDE
    return ((y + sign * ky + SIDE) % SIDE) * SIDE + (x + sign * kx + SIDE) % SIDE


def pieces(value):
    high = value.astype(BF16)
    rest = value - high.astype(F32)
    middle = rest.astype(BF16)
    low = (rest - middle.astype(F32)).astype(BF16)
    return high, middle, low


def to_column(row):
    eye = iota((PAIRS, PAIRS), 0) == iota((PAIRS, PAIRS), 1)
    return jnp.sum(jnp.where(eye, row, 0.0), axis=1, keepdims=True)


def slot_keys(owner_row, me):
    owner_col = to_column(owner_row)
    first = iota((PAIRS, PAIRS), 0)
    second = iota((PAIRS, PAIRS), 1)
    same = owner_col == owner_row
    rank_row = jnp.sum(jnp.where(same & (first < second), 1.0, 0.0), axis=0, keepdims=True)
    rank_col = jnp.sum(jnp.where(same & (second < first), 1.0, 0.0), axis=1, keepdims=True)
    want_row = owner_row * 2.0 + rank_row

    def place(owner, rank):
        whole = owner.astype(jnp.int32)
        y, x = me // SIDE, me % SIDE
        ky = (y - whole // SIDE + SIDE) % SIDE
        kx = (x - whole % SIDE + SIDE) % SIDE
        return ((ky * SIDE + kx) * 2).astype(F32) + rank

    return want_row, place(owner_row, rank_row), place(owner_col, rank_col)


def slot_parts(shape, axis):
    at = iota(shape, axis)
    return at // 8, (at % 8) // 4, (at % 4) // 2, at % 2


def requests(want_rows, row_rows, me):
    k, _, side, rank = slot_parts((SLOTS, PAIRS), 0)
    y, x = me // SIDE, me % SIDE
    owner = ((y - k // SIDE + SIDE) % SIDE) * SIDE + (x - k % SIDE + SIDE) % SIDE
    want = (owner * 2 + rank).astype(F32)
    left = side == 0
    hit = jnp.where(left, want_rows[0], want_rows[1]) == want
    found = jnp.where(hit, jnp.where(left, row_rows[0], row_rows[1]) + 1.0, 0.0)
    return jnp.broadcast_to(jnp.sum(found, axis=1, keepdims=True) - 1.0, (SLOTS, 128))


def pick_matrix(wanted):
    shape = (SLOTS, 4 * ROWS)
    _, half, side, _ = slot_parts(shape, 0)
    lane = iota(shape, 1)
    both = jnp.concatenate([wanted, wanted], axis=1)
    hit = (both == (lane % ROWS).astype(F32)) & (lane // ROWS == half * 2 + side)
    return jnp.where(hit, 1.0, 0.0).astype(BF16)


def pack_matrix(place_cols):
    shape = (4 * PAIRS, SLOTS)
    tall = jnp.concatenate(list(place_cols) * 2, axis=0)
    k, half, side, rank = slot_parts(shape, 1)
    hit = (tall == (k * 2 + rank).astype(F32)) & (iota(shape, 0) // PAIRS == half * 2 + side)
    return jnp.where(hit, 1.0, 0.0).astype(BF16)


def spread_matrix(place_rows):
    shape = (SLOTS, 2 * PAIRS)
    k, half, side, rank = slot_parts(shape, 0)
    wide = [jnp.concatenate([row, row], axis=1) for row in place_rows]
    key = (k * 2 + rank).astype(F32)
    hit = (jnp.where(side == 0, wide[0], wide[1]) == key) & (iota(shape, 1) // PAIRS == half)
    return jnp.where(hit, 1.0, 0.0).astype(BF16)


def dot(a, b):
    return jnp.dot(a, b, preferred_element_type=F32)


def kernel(
    lo_ref, lr_ref, ro_ref, rr_ref, count_ref, gain_ref,
    lt_ref, rt_ref, wq_ref, wk_ref, wv_ref, wo_ref,
    inbox, fin_in,
    table, qkv_w, out_w, outbox, picked, arrived, tokens, scales, resid,
    acc, part, parts_in, fin_out,
    load_sem, idx_s, idx_r, row_s, row_r, ag_s, ag_r, sc_s, sc_r, rs_s, rs_r, fin_s, fin_r,
):
    g = lax.axis_index("group")
    t = lax.axis_index("tensor")
    z, c = t // 2, t % 2
    width = out_w.shape[1]
    half = width // 2
    piece = half // CHUNKS
    share = width // TENSORS

    loads = []

    def load(src, dst):
        copy = pltpu.make_async_copy(src, dst, load_sem.at[len(loads)])
        copy.start()
        loads.append(copy)

    for h in range(2):
        for side, ref in enumerate((lt_ref, rt_ref)):
            load(
                ref.at[:, pl.ds(h * half, half)],
                table.at[pl.ds((h * 2 + side) * ROWS, ROWS), :],
            )

    barrier = pltpu.get_barrier_semaphore()
    for k in range(1, GROUPS):
        pl.semaphore_signal(
            barrier, inc=1, device_id=(group_shift(g, k, 1), t), device_id_type=MESH
        )
    for j in range(1, TENSORS):
        pl.semaphore_signal(
            barrier, inc=1, device_id=(g, (t + j) % TENSORS), device_id_type=MESH
        )

    q_cols = wq_ref.shape[1]
    kv_cols = wk_ref.shape[1]
    load(wq_ref, qkv_w.at[:, pl.ds(0, q_cols)])
    load(wk_ref, qkv_w.at[:, pl.ds(q_cols, kv_cols)])
    load(wv_ref, qkv_w.at[:, pl.ds(q_cols + kv_cols, kv_cols)])
    load(wo_ref, out_w)

    rows = (lr_ref[...].astype(F32), rr_ref[...].astype(F32))
    keys = [slot_keys(ref[...].astype(F32), g) for ref in (lo_ref, ro_ref)]
    asked = requests([key[0] for key in keys], rows, g)
    outbox[...] = asked.reshape(GROUPS, 8, 128)
    pack = pack_matrix([key[2] for key in keys])
    spread = spread_matrix([key[1] for key in keys])

    pl.semaphore_wait(barrier, GROUPS - 1 + TENSORS - 1)

    idx = []
    for k in range(1, GROUPS):
        copy = pltpu.make_async_remote_copy(
            src_ref=outbox.at[k], dst_ref=inbox.at[k],
            send_sem=idx_s.at[k], recv_sem=idx_r.at[k],
            device_id=(group_shift(g, k, -1), t), device_id_type=MESH,
        )
        copy.start()
        idx.append(copy)
    inbox[0] = outbox[0]
    for copy in loads[:4]:
        copy.wait()
    for copy in idx:
        copy.wait_recv()

    pick = pick_matrix(inbox[...].reshape(SLOTS, 128))
    row_copies = []
    for n in range(CHUNKS):
        rows_n = dot(pick, table[:, pl.ds(n * piece, piece)])
        picked[n] = rows_n.astype(BF16).reshape(GROUPS, 8, piece)
        copies = []
        for k in range(1, GROUPS):
            copy = pltpu.make_async_remote_copy(
                src_ref=picked.at[n, k], dst_ref=arrived.at[n, k],
                send_sem=row_s.at[n, k], recv_sem=row_r.at[n, k],
                device_id=(group_shift(g, k, 1), t), device_id_type=MESH,
            )
            copy.start()
            copies.append(copy)
        arrived[n, 0] = picked[n, 0]
        row_copies.append(copies)

    up = ((z + 1) % SIDE) * 2 + c
    down = ((z + SIDE - 1) % SIDE) * 2 + c
    far = ((z + 2) % SIDE) * 2 + c
    twin = z * 2 + 1 - c
    gathers = [{} for _ in range(CHUNKS)]

    def send(n, number, block, side, target):
        place = tokens.at[n, block]
        if side is not None:
            place = place.at[pl.ds(side * 2 * PAIRS, 2 * PAIRS)]
        copy = pltpu.make_async_remote_copy(
            src_ref=place, dst_ref=place,
            send_sem=ag_s.at[n, number], recv_sem=ag_r.at[n, number],
            device_id=(g, target), device_id_type=MESH,
        )
        copy.start()
        gathers[n][number] = copy

    squares = [jnp.zeros((2 * PAIRS, 1), F32)]

    def own(n):
        for copy in row_copies[n]:
            copy.wait_recv()
        got = dot(pack, arrived[n].reshape(SLOTS, piece))
        for h in range(2):
            one = got[h * 2 * PAIRS : (h + 1) * 2 * PAIRS]
            cols = pl.ds(h * half + n * piece, piece)
            squares[0] = squares[0] + jnp.sum(one * one, axis=1, keepdims=True)
            tokens[n, t, pl.ds(h * 2 * PAIRS, 2 * PAIRS), :] = (one * gain_ref[:, cols]).astype(
                BF16
            )
            resid[:, cols] = (one[:PAIRS] + one[PAIRS:]) * (1.0 / 16.0)
        for number, target in ((0, up), (1, down), (2, twin)):
            send(n, number, t, None, target)

    def forward_near(n):
        gathers[n][0].wait_recv()
        send(n, 3, down, 0, up)
        send(n, 4, down, None, twin)
        gathers[n][1].wait_recv()
        send(n, 5, up, 1, down)
        send(n, 6, up, None, twin)

    def forward_far(n):
        gathers[n][3].wait_recv()
        gathers[n][5].wait_recv()
        send(n, 7, far, None, twin)

    depth = 512

    def project(n):
        for number in (2, 4, 6, 7):
            gathers[n][number].wait_recv()

        def block(h, i):
            cols = pl.ds(pl.multiple_of(i * depth, depth), depth)
            a = tokens[n, :, pl.ds(h * 2 * PAIRS, 2 * PAIRS), cols]
            w = qkv_w[pl.ds(pl.multiple_of(h * half + n * piece + i * depth, depth), depth), :]
            return dot(a.reshape(2 * TENSORS * PAIRS, depth), w)

        if n == 0:
            acc[...] = jnp.zeros_like(acc)
        for h in range(2):

            @pl.loop(0, piece // depth)
            def _(i):
                acc[...] += block(h, i)

    factors = []
    for step in range(CHUNKS + 2):
        if step < CHUNKS:
            own(step)
        if step == CHUNKS - 1:
            factor = lax.rsqrt(squares[0] / width + 1e-05)
            scales[t] = jnp.broadcast_to(factor, (2 * PAIRS, 128))
            for j in range(1, TENSORS):
                copy = pltpu.make_async_remote_copy(
                    src_ref=scales.at[t], dst_ref=scales.at[t],
                    send_sem=sc_s.at[j], recv_sem=sc_r.at[j],
                    device_id=(g, ((z + j // 2) % SIDE) * 2 + (c + j % 2) % 2),
                    device_id_type=MESH,
                )
                copy.start()
                factors.append(copy)
        if 0 <= step - 1 < CHUNKS:
            forward_near(step - 1)
        if step - 2 >= 0:
            if step == 2:
                for copy in loads[4:7]:
                    copy.wait()
            forward_far(step - 2)
            project(step - 2)
    for copy in factors:
        copy.wait_recv()

    count = 2 * TENSORS * PAIRS
    factor = scales[...].reshape(count, 128)

    def column(at):
        return acc[:, pl.ds(at * HEAD_DIM, HEAD_DIM)] * factor

    def unit(rows_):
        return (
            rows_ * lax.rsqrt(jnp.mean(rows_ * rows_, axis=-1, keepdims=True) + 1e-06)
        ).astype(BF16)

    heads = q_cols // HEAD_DIM
    key = unit(column(heads))
    value = column(heads + 1).astype(BF16)
    mask = (iota((count, count), 0) % PAIRS) == (iota((count, count), 1) % PAIRS)
    pool = jnp.where(
        iota((PAIRS, count), 0) == iota((PAIRS, count), 1) % PAIRS, 1.0, 0.0
    ).astype(BF16)
    pooled = []
    for head in range(heads):
        query = unit(column(head))
        scores = lax.dot_general(
            query, key, (((1,), (1,)), ((), ())), preferred_element_type=F32
        ) * (SCORE_SCALE / HEAD_DIM)
        expo = jnp.where(mask, jnp.exp(scores), 0.0)
        weights = (expo * (1.0 / jnp.sum(expo, axis=-1, keepdims=True))).astype(BF16)
        context = dot(weights, value).astype(BF16)
        pooled.append(dot(pool, context) * (1.0 / 16.0))
    pooled = jnp.concatenate(pooled, axis=1)
    high = pooled.astype(BF16)
    low = (pooled - high.astype(F32)).astype(BF16)
    both = jnp.concatenate([high, low], axis=0)

    loads[7].wait()
    sums = []
    for j in (4, 5, 2, 3, 6, 7, 1, 0):
        target = ((z + j // 2) % SIDE) * 2 + (c + j % 2) % 2
        cols = pl.ds(pl.multiple_of(target * share, share), share)
        got = dot(both, out_w[:, cols])
        part[j] = got[:PAIRS] + got[PAIRS:] + resid[:, cols]
        if j > 0:
            copy = pltpu.make_async_remote_copy(
                src_ref=part.at[j], dst_ref=parts_in.at[j],
                send_sem=rs_s.at[j], recv_sem=rs_r.at[j],
                device_id=(g, target), device_id_type=MESH,
            )
            copy.start()
            sums.append(copy)
    for copy in sums:
        copy.wait_recv()
    total = part[0]
    for j in range(1, TENSORS):
        total = total + parts_in[j]
    live = iota((PAIRS, share), 0) < count_ref[...]
    total = jnp.where(live, total, 0.0)

    stacked = jnp.concatenate([total[:, : share // 2], total[:, share // 2 :]], axis=0)
    parts3 = pieces(stacked)
    got = dot(spread, parts3[0]) + dot(spread, parts3[1]) + dot(spread, parts3[2])
    fin_out[...] = got.reshape(GROUPS, 8, share // 2)
    finals = []
    for k in range(1, GROUPS):
        copy = pltpu.make_async_remote_copy(
            src_ref=fin_out.at[k], dst_ref=fin_in.at[k],
            send_sem=fin_s.at[k], recv_sem=fin_r.at[k],
            device_id=(group_shift(g, k, -1), t), device_id_type=MESH,
        )
        copy.start()
        finals.append(copy)
    fin_in[0] = fin_out[0]
    for copy in finals:
        copy.wait_recv()

    for copies in [idx, factors, sums, finals] + row_copies:
        for copy in copies:
            copy.wait_send()
    for copies in gathers:
        for copy in copies.values():
            copy.wait_send()


def owner_sums(wanted_ref, came_ref, lout_ref, rout_ref):
    pick = pick_matrix(wanted_ref[...].reshape(SLOTS, 128))
    span = came_ref.shape[2]
    got = jnp.zeros((4 * ROWS, span), F32)
    for one in pieces(came_ref[...].reshape(SLOTS, span)):
        got = got + lax.dot_general(
            pick, one, (((0,), (0,)), ((), ())), preferred_element_type=F32
        )
    for h in range(2):
        for side, out in enumerate((lout_ref, rout_ref)):
            at = (h * 2 + side) * ROWS
            out[:, pl.ds(h * span, span)] = got[at : at + ROWS]


def on_device(
    left_table, right_table, left_owner, left_row, right_owner, right_row, pair_count,
    norm_gain, query_weight, key_weight, value_weight, output_weight,
):
    width = left_table.shape[2]
    half = width // 2
    share = width // TENSORS
    piece = half // CHUNKS
    qkv = query_weight.shape[1] + 2 * key_weight.shape[1]
    vmem = pl.BlockSpec(memory_space=pltpu.VMEM)
    hbm = pl.BlockSpec(memory_space=pl.ANY)
    dma = pltpu.SemaphoreType.DMA
    wanted, came = pl.pallas_call(
        kernel,
        out_shape=(
            jax.ShapeDtypeStruct((GROUPS, 8, 128), F32),
            jax.ShapeDtypeStruct((GROUPS, 8, share // 2), F32),
        ),
        in_specs=[vmem] * 6 + [hbm] * 6,
        out_specs=(vmem, vmem),
        scratch_shapes=[
            pltpu.VMEM((4 * ROWS, half), BF16),
            pltpu.VMEM((width, qkv), BF16),
            pltpu.VMEM(output_weight.shape, BF16),
            pltpu.VMEM((GROUPS, 8, 128), F32),
            pltpu.VMEM((CHUNKS, GROUPS, 8, piece), BF16),
            pltpu.VMEM((CHUNKS, GROUPS, 8, piece), BF16),
            pltpu.VMEM((CHUNKS, TENSORS, 4 * PAIRS, piece), BF16),
            pltpu.VMEM((TENSORS, 2 * PAIRS, 128), F32),
            pltpu.VMEM((PAIRS, width), F32),
            pltpu.VMEM((2 * TENSORS * PAIRS, qkv), F32),
            pltpu.VMEM((TENSORS, PAIRS, share), F32),
            pltpu.VMEM((TENSORS, PAIRS, share), F32),
            pltpu.VMEM((GROUPS, 8, share // 2), F32),
            dma((8,)),
            dma((GROUPS,)), dma((GROUPS,)),
            dma((CHUNKS, GROUPS)), dma((CHUNKS, GROUPS)),
            dma((CHUNKS, 8)), dma((CHUNKS, 8)),
            dma((TENSORS,)), dma((TENSORS,)),
            dma((TENSORS,)), dma((TENSORS,)),
            dma((GROUPS,)), dma((GROUPS,)),
        ],
        compiler_params=pltpu.CompilerParams(
            collective_id=0, has_side_effects=True, vmem_limit_bytes=56 * 1024 * 1024
        ),
    )(
        left_owner.reshape(1, PAIRS), left_row.reshape(1, PAIRS),
        right_owner.reshape(1, PAIRS), right_row.reshape(1, PAIRS),
        pair_count.reshape(1, 1), norm_gain.reshape(1, width),
        left_table.reshape(ROWS, width), right_table.reshape(ROWS, width),
        query_weight, key_weight, value_weight, output_weight,
    )
    out = jax.ShapeDtypeStruct((ROWS, share), F32)
    return pl.pallas_call(
        owner_sums, out_shape=(out, out), in_specs=[vmem, vmem], out_specs=(vmem, vmem)
    )(wanted, came)


def solution(mesh):
    return jax.shard_map(
        on_device,
        mesh=mesh,
        in_specs=(
            P("group", "tensor", None), P("group", "tensor", None),
            P("group", None), P("group"), P("group", None), P("group"), P("group"), P(),
            P(None, "tensor"), P(None, "tensor"), P(None, "tensor"), P("tensor", None),
        ),
        out_specs=(P("group", "tensor"), P("group", "tensor")),
        check_vma=False,
    )
```

```python
import jax
import jax.numpy as jnp
from jax import lax
from jax.experimental import pallas as pl
from jax.experimental.pallas import tpu as pltpu
from jax.sharding import PartitionSpec as P

HEAD_DIM = 128
SCORE_SCALE = 4.0
MESH = pl.DeviceIdType.MESH
GROUPS = 16
SIDE = 4
TENSORS = 8
PAIRS = 16
SLOTS = GROUPS * 8
ROWS = 64
CHUNKS = 4
AHEAD = 4
LAG_NEAR = 1
LAG_FAR = 2
LAG_PROJECT = 3
ORDER = sorted(
    range(1, GROUPS),
    key=lambda k: -(min(k // SIDE, SIDE - k // SIDE) + min(k % SIDE, SIDE - k % SIDE)),
)
F32 = jnp.float32
BF16 = jnp.bfloat16


def iota(shape, axis):
    return lax.broadcasted_iota(jnp.int32, shape, axis)


def group_shift(g, k, sign):
    y, x = g // SIDE, g % SIDE
    ky, kx = k // SIDE, k % SIDE
    return ((y + sign * ky + SIDE) % SIDE) * SIDE + (x + sign * kx + SIDE) % SIDE


def pieces(value):
    high = value.astype(BF16)
    rest = value - high.astype(F32)
    middle = rest.astype(BF16)
    low = (rest - middle.astype(F32)).astype(BF16)
    return high, middle, low


def to_column(row):
    eye = iota((PAIRS, PAIRS), 0) == iota((PAIRS, PAIRS), 1)
    return jnp.sum(jnp.where(eye, row, 0.0), axis=1, keepdims=True)


def slot_keys(owner_row, me):
    owner_col = to_column(owner_row)
    first = iota((PAIRS, PAIRS), 0)
    second = iota((PAIRS, PAIRS), 1)
    same = owner_col == owner_row
    rank_row = jnp.sum(jnp.where(same & (first < second), 1.0, 0.0), axis=0, keepdims=True)
    rank_col = jnp.sum(jnp.where(same & (second < first), 1.0, 0.0), axis=1, keepdims=True)
    want_row = owner_row * 2.0 + rank_row

    def place(owner, rank):
        whole = owner.astype(jnp.int32)
        y, x = me // SIDE, me % SIDE
        ky = (y - whole // SIDE + SIDE) % SIDE
        kx = (x - whole % SIDE + SIDE) % SIDE
        return ((ky * SIDE + kx) * 2).astype(F32) + rank

    return want_row, place(owner_row, rank_row), place(owner_col, rank_col)


def slot_parts(shape, axis):
    at = iota(shape, axis)
    return at // 8, (at % 8) // 4, (at % 4) // 2, at % 2


def requests(want_rows, row_rows, me):
    k, _, side, rank = slot_parts((SLOTS, PAIRS), 0)
    y, x = me // SIDE, me % SIDE
    owner = ((y - k // SIDE + SIDE) % SIDE) * SIDE + (x - k % SIDE + SIDE) % SIDE
    want = (owner * 2 + rank).astype(F32)
    left = side == 0
    hit = jnp.where(left, want_rows[0], want_rows[1]) == want
    found = jnp.where(hit, jnp.where(left, row_rows[0], row_rows[1]) + 1.0, 0.0)
    return jnp.broadcast_to(jnp.sum(found, axis=1, keepdims=True) - 1.0, (SLOTS, 128))


def pick_matrix(wanted):
    shape = (SLOTS, 4 * ROWS)
    _, half, side, _ = slot_parts(shape, 0)
    lane = iota(shape, 1)
    both = jnp.concatenate([wanted, wanted], axis=1)
    hit = (both == (lane % ROWS).astype(F32)) & (lane // ROWS == half * 2 + side)
    return jnp.where(hit, 1.0, 0.0).astype(BF16)


def pack_matrix(place_cols):
    shape = (4 * PAIRS, SLOTS)
    tall = jnp.concatenate(list(place_cols) * 2, axis=0)
    k, half, side, rank = slot_parts(shape, 1)
    hit = (tall == (k * 2 + rank).astype(F32)) & (iota(shape, 0) // PAIRS == half * 2 + side)
    return jnp.where(hit, 1.0, 0.0).astype(BF16)


def spread_matrix(place_rows):
    shape = (SLOTS, 2 * PAIRS)
    k, half, side, rank = slot_parts(shape, 0)
    wide = [jnp.concatenate([row, row], axis=1) for row in place_rows]
    key = (k * 2 + rank).astype(F32)
    hit = (jnp.where(side == 0, wide[0], wide[1]) == key) & (iota(shape, 1) // PAIRS == half)
    return jnp.where(hit, 1.0, 0.0).astype(BF16)


def dot(a, b):
    return jnp.dot(a, b, preferred_element_type=F32)


def kernel(
    lo_hbm, lr_hbm, ro_hbm, rr_hbm, count_hbm, gain_hbm,
    lt_ref, rt_ref, wq_ref, wk_ref, wv_ref, wo_ref,
    wanted, fin_in,
    lo_ref, lr_ref, ro_ref, rr_ref, count_ref, gain_ref, inbox,
    table, qkv_w, out_w, outbox, picked, arrived, tokens, scales, resid,
    acc, across, across_in, part, parts_in, fin_out,
    load_sem, idx_s, idx_r, row_s, row_r, ag_s, ag_r, sc_s, sc_r, tw_s, tw_r, rs_s, rs_r,
    fin_s, fin_r,
):
    g = lax.axis_index("group")
    t = lax.axis_index("tensor")
    z, c = t // 2, t % 2
    width = out_w.shape[1]
    half = width // 2
    piece = half // CHUNKS
    share = width // TENSORS

    loads = []

    def load(src, dst):
        copy = pltpu.make_async_copy(src, dst, load_sem.at[len(loads)])
        copy.start()
        loads.append(copy)

    for src, dst in (
        (lo_hbm, lo_ref), (lr_hbm, lr_ref), (ro_hbm, ro_ref), (rr_hbm, rr_ref)
    ):
        load(src, dst)
    for h in range(2):
        for side, ref in enumerate((lt_ref, rt_ref)):
            load(
                ref.at[:, pl.ds(h * half, half)],
                table.at[pl.ds((h * 2 + side) * ROWS, ROWS), :],
            )

    barrier = pltpu.get_barrier_semaphore()
    for k in ORDER:
        pl.semaphore_signal(
            barrier, inc=1, device_id=(group_shift(g, k, 1), t), device_id_type=MESH
        )
    for j in range(1, TENSORS):
        pl.semaphore_signal(
            barrier, inc=1, device_id=(g, (t + j) % TENSORS), device_id_type=MESH
        )

    q_cols = wq_ref.shape[1]
    kv_cols = wk_ref.shape[1]
    load(gain_hbm, gain_ref)
    load(count_hbm, count_ref)
    load(wq_ref, qkv_w.at[:, pl.ds(0, q_cols)])
    load(wk_ref, qkv_w.at[:, pl.ds(q_cols, kv_cols)])
    load(wv_ref, qkv_w.at[:, pl.ds(q_cols + kv_cols, kv_cols)])
    load(wo_ref, out_w)

    for copy in loads[:4]:
        copy.wait()
    rows = (lr_ref[...].astype(F32), rr_ref[...].astype(F32))
    keys = [slot_keys(ref[...].astype(F32), g) for ref in (lo_ref, ro_ref)]
    asked = requests([key[0] for key in keys], rows, g)
    outbox[...] = asked.reshape(GROUPS, 8, 128)
    pack = pack_matrix([key[2] for key in keys])
    spread = spread_matrix([key[1] for key in keys])

    pl.semaphore_wait(barrier, GROUPS - 1 + TENSORS - 1)

    idx = []
    for k in ORDER:
        copy = pltpu.make_async_remote_copy(
            src_ref=outbox.at[k], dst_ref=inbox.at[k],
            send_sem=idx_s.at[k], recv_sem=idx_r.at[k],
            device_id=(group_shift(g, k, -1), t), device_id_type=MESH,
        )
        copy.start()
        idx.append(copy)
    inbox[0] = outbox[0]
    for copy in loads[4:10]:
        copy.wait()
    for copy in idx:
        copy.wait_recv()
    load(inbox, wanted)

    pick = pick_matrix(inbox[...].reshape(SLOTS, 128))
    def ask(n):
        for k in ORDER:
            copy = pltpu.make_async_remote_copy(
                src_ref=picked.at[n, k], dst_ref=arrived.at[n, k],
                send_sem=row_s.at[n, k], recv_sem=row_r.at[n, k],
                device_id=(group_shift(g, k, 1), t), device_id_type=MESH,
            )
            copy.start()
            copies[n].append(copy)

    copies = [[] for _ in range(CHUNKS)]
    for n in range(CHUNKS):
        rows_n = dot(pick, table[:, pl.ds(n * piece, piece)])
        picked[n] = rows_n.astype(BF16).reshape(GROUPS, 8, piece)
        if n < AHEAD:
            ask(n)
        arrived[n, 0] = picked[n, 0]
    row_copies = copies

    up = ((z + 1) % SIDE) * 2 + c
    down = ((z + SIDE - 1) % SIDE) * 2 + c
    far = ((z + 2) % SIDE) * 2 + c
    twin = z * 2 + 1 - c
    gathers = [{} for _ in range(CHUNKS)]

    def send(n, number, block, side, target):
        place = tokens.at[n, block]
        if side is not None:
            place = place.at[pl.ds(side * 2 * PAIRS, 2 * PAIRS)]
        copy = pltpu.make_async_remote_copy(
            src_ref=place, dst_ref=place,
            send_sem=ag_s.at[n, number], recv_sem=ag_r.at[n, number],
            device_id=(g, target), device_id_type=MESH,
        )
        copy.start()
        gathers[n][number] = copy

    squares = [jnp.zeros((2 * PAIRS, 1), F32)]

    def own(n):
        for copy in row_copies[n]:
            copy.wait_recv()
        if n + AHEAD < CHUNKS:
            ask(n + AHEAD)
        got = dot(pack, arrived[n].reshape(SLOTS, piece))
        for h in range(2):
            one = got[h * 2 * PAIRS : (h + 1) * 2 * PAIRS]
            cols = pl.ds(h * half + n * piece, piece)
            squares[0] = squares[0] + jnp.sum(one * one, axis=1, keepdims=True)
            tokens[n, t, pl.ds(h * 2 * PAIRS, 2 * PAIRS), :] = (one * gain_ref[:, cols]).astype(
                BF16
            )
            resid[:, cols] = (one[:PAIRS] + one[PAIRS:]) * (1.0 / 16.0)
        for number, target in ((0, up), (1, down), (2, twin)):
            send(n, number, t, None, target)

    def forward_near(n):
        gathers[n][0].wait_recv()
        send(n, 3, down, 0, up)
        send(n, 4, down, None, twin)
        gathers[n][1].wait_recv()
        send(n, 5, up, 1, down)
        send(n, 6, up, None, twin)

    def forward_far(n):
        gathers[n][3].wait_recv()
        gathers[n][5].wait_recv()
        send(n, 7, far, None, twin)

    depth = 512

    def project(n):
        for number in (2, 4, 6, 7):
            gathers[n][number].wait_recv()

        def block(h, i):
            cols = pl.ds(pl.multiple_of(i * depth, depth), depth)
            a = tokens[n, :, pl.ds(h * 2 * PAIRS, 2 * PAIRS), cols]
            w = qkv_w[pl.ds(pl.multiple_of(h * half + n * piece + i * depth, depth), depth), :]
            return dot(a.reshape(2 * TENSORS * PAIRS, depth), w)

        if n == 0:
            acc[...] = jnp.zeros_like(acc)
        for h in range(2):

            @pl.loop(0, piece // depth)
            def _(i):
                acc[...] += block(h, i)

    factors = []
    for step in range(CHUNKS + LAG_PROJECT):
        if step < CHUNKS:
            own(step)
        if step == CHUNKS - 1:
            factor = lax.rsqrt(squares[0] / width + 1e-05)
            scales[t] = jnp.broadcast_to(factor, (2 * PAIRS, 128))
            for j in range(1, TENSORS):
                copy = pltpu.make_async_remote_copy(
                    src_ref=scales.at[t], dst_ref=scales.at[t],
                    send_sem=sc_s.at[j], recv_sem=sc_r.at[j],
                    device_id=(g, ((z + j // 2) % SIDE) * 2 + (c + j % 2) % 2),
                    device_id_type=MESH,
                )
                copy.start()
                factors.append(copy)
        if 0 <= step - LAG_NEAR < CHUNKS:
            forward_near(step - LAG_NEAR)
        if 0 <= step - LAG_FAR < CHUNKS:
            forward_far(step - LAG_FAR)
        if step >= LAG_PROJECT:
            if step == LAG_PROJECT:
                for copy in loads[10:13]:
                    copy.wait()
            project(step - LAG_PROJECT)
    for copy in factors:
        copy.wait_recv()

    count = 2 * TENSORS * PAIRS
    factor = scales[...].reshape(count, 128)

    def column(at):
        return acc[:, pl.ds(at * HEAD_DIM, HEAD_DIM)] * factor

    def unit(rows_):
        return (
            rows_ * lax.rsqrt(jnp.mean(rows_ * rows_, axis=-1, keepdims=True) + 1e-06)
        ).astype(BF16)

    heads = q_cols // HEAD_DIM
    key = unit(column(heads))
    value = column(heads + 1).astype(BF16)
    mask = (iota((count, count), 0) % PAIRS) == (iota((count, count), 1) % PAIRS)
    pool = jnp.where(
        iota((PAIRS, count), 0) == iota((PAIRS, count), 1) % PAIRS, 1.0, 0.0
    ).astype(BF16)
    pooled = []
    for head in range(heads):
        query = unit(column(head))
        scores = lax.dot_general(
            query, key, (((1,), (1,)), ((), ())), preferred_element_type=F32
        ) * (SCORE_SCALE / HEAD_DIM)
        expo = jnp.where(mask, jnp.exp(scores), 0.0)
        weights = (expo * (1.0 / jnp.sum(expo, axis=-1, keepdims=True))).astype(BF16)
        context = dot(weights, value).astype(BF16)
        pooled.append(dot(pool, context) * (1.0 / 16.0))
    pooled = jnp.concatenate(pooled, axis=1)
    high = pooled.astype(BF16)
    low = (pooled - high.astype(F32)).astype(BF16)
    both = jnp.concatenate([high, low], axis=0)

    loads[13].wait()
    sums = []

    def partial(dz, core):
        cols = pl.ds(pl.multiple_of((((z + dz) % SIDE) * 2 + core) * share, share), share)
        got = dot(both, out_w[:, cols])
        return got[:PAIRS] + got[PAIRS:] + resid[:, cols]

    def push(source, target_ref, sends, recvs, at, target):
        copy = pltpu.make_async_remote_copy(
            src_ref=source.at[at], dst_ref=target_ref.at[at],
            send_sem=sends.at[at], recv_sem=recvs.at[at],
            device_id=(g, target), device_id_type=MESH,
        )
        copy.start()
        sums.append(copy)
        return copy

    crossing = {}
    for dz in (2, 1, 3, 0):
        across[dz] = partial(dz, 1 - c)
        crossing[dz] = push(across, across_in, tw_s, tw_r, dz, twin)
    coming = []
    for dz in (2, 1, 3, 0):
        mine = partial(dz, c)
        crossing[dz].wait_recv()
        part[dz] = mine + across_in[dz]
        if dz > 0:
            coming.append(push(part, parts_in, rs_s, rs_r, dz, ((z + dz) % SIDE) * 2 + c))
    for copy in coming:
        copy.wait_recv()
    total = part[0] + parts_in[1] + parts_in[2] + parts_in[3]
    live = iota((PAIRS, share), 0) < count_ref[...]
    total = jnp.where(live, total, 0.0)

    stacked = jnp.concatenate([total[:, : share // 2], total[:, share // 2 :]], axis=0)
    parts3 = pieces(stacked)
    got = dot(spread, parts3[0]) + dot(spread, parts3[1]) + dot(spread, parts3[2])
    fin_out[...] = got.reshape(GROUPS, 8, share // 2)
    finals = []
    for k in ORDER:
        copy = pltpu.make_async_remote_copy(
            src_ref=fin_out.at[k], dst_ref=fin_in.at[k],
            send_sem=fin_s.at[k], recv_sem=fin_r.at[k],
            device_id=(group_shift(g, k, -1), t), device_id_type=MESH,
        )
        copy.start()
        finals.append(copy)
    load(fin_out.at[0], fin_in.at[0])
    for copy in finals:
        copy.wait_recv()

    for copy in loads[14:]:
        copy.wait()
    for copies in [idx, factors, sums, finals] + row_copies:
        for copy in copies:
            copy.wait_send()
    for copies in gathers:
        for copy in copies.values():
            copy.wait_send()


def owner_sums(wanted_ref, came_ref, lout_ref, rout_ref):
    pick = pick_matrix(wanted_ref[...].reshape(SLOTS, 128))
    span = came_ref.shape[2]
    got = jnp.zeros((4 * ROWS, span), F32)
    for one in pieces(came_ref[...].reshape(SLOTS, span)):
        got = got + lax.dot_general(
            pick, one, (((0,), (0,)), ((), ())), preferred_element_type=F32
        )
    for h in range(2):
        for side, out in enumerate((lout_ref, rout_ref)):
            at = (h * 2 + side) * ROWS
            out[:, pl.ds(h * span, span)] = got[at : at + ROWS]


def on_device(
    left_table, right_table, left_owner, left_row, right_owner, right_row, pair_count,
    norm_gain, query_weight, key_weight, value_weight, output_weight,
):
    width = left_table.shape[2]
    half = width // 2
    share = width // TENSORS
    piece = half // CHUNKS
    qkv = query_weight.shape[1] + 2 * key_weight.shape[1]
    vmem = pl.BlockSpec(memory_space=pltpu.VMEM)
    hbm = pl.BlockSpec(memory_space=pl.ANY)
    dma = pltpu.SemaphoreType.DMA
    wanted, came = pl.pallas_call(
        kernel,
        out_shape=(
            jax.ShapeDtypeStruct((GROUPS, 8, 128), F32),
            jax.ShapeDtypeStruct((GROUPS, 8, share // 2), F32),
        ),
        in_specs=[hbm] * 12,
        out_specs=(hbm, hbm),
        scratch_shapes=[
            pltpu.VMEM((1, PAIRS), jnp.int32),
            pltpu.VMEM((1, PAIRS), jnp.int32),
            pltpu.VMEM((1, PAIRS), jnp.int32),
            pltpu.VMEM((1, PAIRS), jnp.int32),
            pltpu.VMEM((1, 1), jnp.int32),
            pltpu.VMEM((1, width), F32),
            pltpu.VMEM((GROUPS, 8, 128), F32),
            pltpu.VMEM((4 * ROWS, half), BF16),
            pltpu.VMEM((width, qkv), BF16),
            pltpu.VMEM(output_weight.shape, BF16),
            pltpu.VMEM((GROUPS, 8, 128), F32),
            pltpu.VMEM((CHUNKS, GROUPS, 8, piece), BF16),
            pltpu.VMEM((CHUNKS, GROUPS, 8, piece), BF16),
            pltpu.VMEM((CHUNKS, TENSORS, 4 * PAIRS, piece), BF16),
            pltpu.VMEM((TENSORS, 2 * PAIRS, 128), F32),
            pltpu.VMEM((PAIRS, width), F32),
            pltpu.VMEM((2 * TENSORS * PAIRS, qkv), F32),
            pltpu.VMEM((SIDE, PAIRS, share), F32),
            pltpu.VMEM((SIDE, PAIRS, share), F32),
            pltpu.VMEM((SIDE, PAIRS, share), F32),
            pltpu.VMEM((SIDE, PAIRS, share), F32),
            pltpu.VMEM((GROUPS, 8, share // 2), F32),
            dma((16,)),
            dma((GROUPS,)), dma((GROUPS,)),
            dma((CHUNKS, GROUPS)), dma((CHUNKS, GROUPS)),
            dma((CHUNKS, 8)), dma((CHUNKS, 8)),
            dma((TENSORS,)), dma((TENSORS,)),
            dma((SIDE,)), dma((SIDE,)),
            dma((SIDE,)), dma((SIDE,)),
            dma((GROUPS,)), dma((GROUPS,)),
        ],
        compiler_params=pltpu.CompilerParams(
            collective_id=0, has_side_effects=True, vmem_limit_bytes=56 * 1024 * 1024
        ),
    )(
        left_owner.reshape(1, PAIRS), left_row.reshape(1, PAIRS),
        right_owner.reshape(1, PAIRS), right_row.reshape(1, PAIRS),
        pair_count.reshape(1, 1), norm_gain.reshape(1, width),
        left_table.reshape(ROWS, width), right_table.reshape(ROWS, width),
        query_weight, key_weight, value_weight, output_weight,
    )
    out = jax.ShapeDtypeStruct((ROWS, share), F32)
    return pl.pallas_call(
        owner_sums, out_shape=(out, out), in_specs=[vmem, vmem], out_specs=(vmem, vmem)
    )(wanted, came)


def solution(mesh):
    return jax.shard_map(
        on_device,
        mesh=mesh,
        in_specs=(
            P("group", "tensor", None), P("group", "tensor", None),
            P("group", None), P("group"), P("group", None), P("group"), P("group"), P(),
            P(None, "tensor"), P(None, "tensor"), P(None, "tensor"), P("tensor", None),
        ),
        out_specs=(P("group", "tensor"), P("group", "tensor")),
        check_vma=False,
    )
```

```python
import jax
import jax.numpy as jnp
from jax import lax
from jax.experimental import pallas as pl
from jax.experimental.pallas import tpu as pltpu
from jax.sharding import PartitionSpec as P

HEAD_DIM = 128
SCORE_SCALE = 4.0
MESH = pl.DeviceIdType.MESH
GROUPS = 16
SIDE = 4
TENSORS = 8
PAIRS = 16
SLOTS = GROUPS * 8
ROWS = 64
PIECES = (1024, 1024, 1024, 1024)
STARTS = tuple(sum(PIECES[:n]) for n in range(len(PIECES)))
CHUNKS = len(PIECES)
LEAD = 128
AHEAD = 4
LAG_NEAR = 1
LAG_FAR = 2
LAG_PROJECT = 3
ORDER = sorted(
    range(1, GROUPS),
    key=lambda k: -(min(k // SIDE, SIDE - k // SIDE) + min(k % SIDE, SIDE - k % SIDE)),
)
F32 = jnp.float32
BF16 = jnp.bfloat16


def iota(shape, axis):
    return lax.broadcasted_iota(jnp.int32, shape, axis)


def group_shift(g, k, sign):
    y, x = g // SIDE, g % SIDE
    ky, kx = k // SIDE, k % SIDE
    return ((y + sign * ky + SIDE) % SIDE) * SIDE + (x + sign * kx + SIDE) % SIDE


def pieces(value):
    high = value.astype(BF16)
    rest = value - high.astype(F32)
    middle = rest.astype(BF16)
    low = (rest - middle.astype(F32)).astype(BF16)
    return high, middle, low


def to_column(row):
    eye = iota((PAIRS, PAIRS), 0) == iota((PAIRS, PAIRS), 1)
    return jnp.sum(jnp.where(eye, row, 0.0), axis=1, keepdims=True)


def slot_keys(owner_row, me):
    owner_col = to_column(owner_row)
    first = iota((PAIRS, PAIRS), 0)
    second = iota((PAIRS, PAIRS), 1)
    same = owner_col == owner_row
    rank_row = jnp.sum(jnp.where(same & (first < second), 1.0, 0.0), axis=0, keepdims=True)
    rank_col = jnp.sum(jnp.where(same & (second < first), 1.0, 0.0), axis=1, keepdims=True)
    want_row = owner_row * 2.0 + rank_row

    def place(owner, rank):
        whole = owner.astype(jnp.int32)
        y, x = me // SIDE, me % SIDE
        ky = (y - (whole >> 2)) & 3
        kx = (x - whole) & 3
        return ((ky * SIDE + kx) * 2).astype(F32) + rank

    return want_row, place(owner_row, rank_row), place(owner_col, rank_col)


def slot_parts(shape, axis):
    at = iota(shape, axis)
    return at >> 3, (at >> 2) & 1, (at >> 1) & 1, at & 1


def requests(want_rows, row_rows, me):
    k, _, side, rank = slot_parts((SLOTS, PAIRS), 0)
    y, x = me // SIDE, me % SIDE
    owner = (((y - (k >> 2)) & 3) << 2) + ((x - k) & 3)
    want = (owner * 2 + rank).astype(F32)
    left = side == 0
    hit = jnp.where(left, want_rows[0], want_rows[1]) == want
    found = jnp.where(hit, jnp.where(left, row_rows[0], row_rows[1]) + 1.0, 0.0)
    return jnp.broadcast_to(jnp.sum(found, axis=1, keepdims=True) - 1.0, (SLOTS, 128))


def pick_matrix(wanted):
    shape = (SLOTS, 4 * ROWS)
    _, half, side, _ = slot_parts(shape, 0)
    lane = iota(shape, 1)
    both = jnp.concatenate([wanted, wanted], axis=1)
    hit = (both == (lane & 63).astype(F32)) & ((lane >> 6) == half * 2 + side)
    return jnp.where(hit, 1.0, 0.0).astype(BF16)


def pack_matrix(place_cols):
    shape = (4 * PAIRS, SLOTS)
    tall = jnp.concatenate(list(place_cols) * 2, axis=0)
    k, half, side, rank = slot_parts(shape, 1)
    hit = (tall == (k * 2 + rank).astype(F32)) & ((iota(shape, 0) >> 4) == half * 2 + side)
    return jnp.where(hit, 1.0, 0.0).astype(BF16)


def spread_matrix(place_rows):
    shape = (SLOTS, 2 * PAIRS)
    k, half, side, rank = slot_parts(shape, 0)
    wide = [jnp.concatenate([row, row], axis=1) for row in place_rows]
    key = (k * 2 + rank).astype(F32)
    hit = (jnp.where(side == 0, wide[0], wide[1]) == key) & ((iota(shape, 1) >> 4) == half)
    return jnp.where(hit, 1.0, 0.0).astype(BF16)


def dot(a, b):
    return jnp.dot(a, b, preferred_element_type=F32)


def kernel(
    lo_hbm, lr_hbm, ro_hbm, rr_hbm, count_hbm, gain_hbm,
    lt_ref, rt_ref, wq_ref, wk_ref, wv_ref, wo_ref,
    wanted, fin_in,
    lo_ref, lr_ref, ro_ref, rr_ref, count_ref, gain_ref, inbox,
    table, qkv_w, out_w, outbox, picked, arrived, resid,
    acc, across, across_in, part, parts_in, fin_out,
    load_sem, idx_s, idx_r, row_s, row_r, ag_s, ag_r, tw_s, tw_r, rs_s, rs_r,
    fin_s, fin_r, *tokens,
):
    g = lax.axis_index("group")
    t = lax.axis_index("tensor")
    z, c = t // 2, t % 2
    width = out_w.shape[1]
    half = width // 2
    share = width // TENSORS

    barrier = pltpu.get_barrier_semaphore()
    for k in ORDER:
        pl.semaphore_signal(
            barrier, inc=1, device_id=(group_shift(g, k, 1), t), device_id_type=MESH
        )
    for j in range(1, TENSORS):
        pl.semaphore_signal(
            barrier, inc=1, device_id=(g, (t + j) % TENSORS), device_id_type=MESH
        )

    loads = []

    def load(src, dst):
        copy = pltpu.make_async_copy(src, dst, load_sem.at[len(loads)])
        copy.start()
        loads.append(copy)

    for src, dst in (
        (lo_hbm, lo_ref), (lr_hbm, lr_ref), (ro_hbm, ro_ref), (rr_hbm, rr_ref)
    ):
        load(src, dst)
    for h in range(2):
        for side, ref in enumerate((lt_ref, rt_ref)):
            load(
                ref.at[:, pl.ds(h * half, half)],
                table.at[pl.ds((h * 2 + side) * ROWS, ROWS), pl.ds(LEAD, half)],
            )

    q_cols = wq_ref.shape[1]
    kv_cols = wk_ref.shape[1]
    load(gain_hbm, gain_ref)
    load(count_hbm, count_ref)
    load(wq_ref, qkv_w.at[:, pl.ds(0, q_cols)])
    load(wk_ref, qkv_w.at[:, pl.ds(q_cols, kv_cols)])
    load(wv_ref, qkv_w.at[:, pl.ds(q_cols + kv_cols, kv_cols)])
    load(wo_ref, out_w)

    for copy in loads[:4]:
        copy.wait()
    rows = (lr_ref[...].astype(F32), rr_ref[...].astype(F32))
    keys = [slot_keys(ref[...].astype(F32), g) for ref in (lo_ref, ro_ref)]
    asked = requests([key[0] for key in keys], rows, g)
    outbox[...] = asked.reshape(GROUPS, 8, 128)
    pack = pack_matrix([key[2] for key in keys])
    spread = spread_matrix([key[1] for key in keys])

    pl.semaphore_wait(barrier, GROUPS - 1 + TENSORS - 1)

    idx = []
    for k in ORDER:
        copy = pltpu.make_async_remote_copy(
            src_ref=outbox.at[k], dst_ref=inbox.at[k],
            send_sem=idx_s.at[k], recv_sem=idx_r.at[k],
            device_id=(group_shift(g, k, -1), t), device_id_type=MESH,
        )
        copy.start()
        idx.append(copy)
    inbox[0] = outbox[0]
    for copy in loads[4:10]:
        copy.wait()
    block = half // 8

    def squares(i, sums):
        at = pl.ds(pl.multiple_of(LEAD + i * block, 128), block)
        values = table[:, at].astype(F32)
        values = values * values
        for n in range(block // 128):
            sums = sums + values[:, n * 128 : (n + 1) * 128]
        return sums

    sums = lax.fori_loop(0, 8, squares, jnp.zeros((4 * ROWS, 128), F32))
    sums = jnp.sum(sums[: 2 * ROWS] + sums[2 * ROWS :], axis=1, keepdims=True)
    lane = iota((2 * ROWS, LEAD), 1)
    lead = jnp.zeros((2 * ROWS, LEAD), F32)
    for n, one in enumerate(pieces(lax.rsqrt(sums / width + 1e-05))):
        lead = jnp.where(lane == n, one.astype(F32), lead)
    lead = lead.astype(BF16)
    table[pl.ds(0, 2 * ROWS), pl.ds(0, LEAD)] = lead
    table[pl.ds(2 * ROWS, 2 * ROWS), pl.ds(0, LEAD)] = lead
    for copy in idx:
        copy.wait_recv()
    load(inbox, wanted)

    pick = pick_matrix(inbox[...].reshape(SLOTS, 128))
    def chunk(n):
        return pl.ds(0, LEAD + PIECES[0]) if n == 0 else pl.ds(LEAD + STARTS[n], PIECES[n])

    def ask(n):
        span = chunk(n)
        for k in ORDER:
            copy = pltpu.make_async_remote_copy(
                src_ref=picked.at[k, :, span], dst_ref=arrived.at[k, :, span],
                send_sem=row_s.at[n, k], recv_sem=row_r.at[n, k],
                device_id=(group_shift(g, k, 1), t), device_id_type=MESH,
            )
            copy.start()
            copies[n].append(copy)

    copies = [[] for _ in range(CHUNKS)]
    for n in range(CHUNKS):
        span = chunk(n)
        rows_n = dot(pick, table[:, span])
        picked[:, :, span] = rows_n.astype(BF16).reshape(GROUPS, 8, span.size)
        if n < AHEAD:
            ask(n)
        arrived[0, :, span] = picked[0, :, span]
    row_copies = copies

    up = ((z + 1) % SIDE) * 2 + c
    down = ((z + SIDE - 1) % SIDE) * 2 + c
    far = ((z + 2) % SIDE) * 2 + c
    twin = z * 2 + 1 - c
    gathers = [{} for _ in range(CHUNKS)]

    def send(n, number, block, side, target):
        place = tokens[n].at[block]
        if side is not None:
            place = place.at[pl.ds(side * 2 * PAIRS, 2 * PAIRS)]
        copy = pltpu.make_async_remote_copy(
            src_ref=place, dst_ref=place,
            send_sem=ag_s.at[n, number], recv_sem=ag_r.at[n, number],
            device_id=(g, target), device_id_type=MESH,
        )
        copy.start()
        gathers[n][number] = copy

    factor = []

    def own(n):
        for copy in row_copies[n]:
            copy.wait_recv()
        if n + AHEAD < CHUNKS:
            ask(n + AHEAD)
        piece = PIECES[n]
        if n == 0:
            led = dot(pack, arrived[:, :, pl.ds(0, LEAD)].reshape(SLOTS, LEAD))
            led = led[: 2 * PAIRS]
            factor.append(led[:, 0:1] + led[:, 1:2] + led[:, 2:3])
        got = dot(pack, arrived[:, :, pl.ds(LEAD + STARTS[n], piece)].reshape(SLOTS, piece))
        for h in range(2):
            one = got[h * 2 * PAIRS : (h + 1) * 2 * PAIRS]
            cols = pl.ds(h * half + STARTS[n], piece)
            tokens[n][t, pl.ds(h * 2 * PAIRS, 2 * PAIRS), :] = (
                one * factor[0] * gain_ref[:, cols]
            ).astype(BF16)
            resid[:, cols] = (one[:PAIRS] + one[PAIRS:]) * (1.0 / 16.0)
        for number, target in ((0, up), (1, down), (2, twin)):
            send(n, number, t, None, target)

    def forward_near(n):
        gathers[n][0].wait_recv()
        send(n, 3, down, 0, up)
        send(n, 4, down, None, twin)
        gathers[n][1].wait_recv()
        send(n, 5, up, 1, down)
        send(n, 6, up, None, twin)

    def forward_far(n):
        gathers[n][3].wait_recv()
        gathers[n][5].wait_recv()
        send(n, 7, far, None, twin)

    def project(n):
        for number in (2, 4, 6, 7):
            gathers[n][number].wait_recv()
        depth = 512 if PIECES[n] % 512 == 0 else 256

        def block(h, i):
            cols = pl.ds(pl.multiple_of(i * depth, depth), depth)
            a = tokens[n][:, pl.ds(h * 2 * PAIRS, 2 * PAIRS), cols]
            start = pl.multiple_of(h * half + STARTS[n] + i * depth, 256)
            w = qkv_w[pl.ds(start, depth), :]
            return dot(a.reshape(2 * TENSORS * PAIRS, depth), w)

        if n == 0:
            acc[...] = jnp.zeros_like(acc)
        for h in range(2):

            @pl.loop(0, PIECES[n] // depth)
            def _(i):
                acc[...] += block(h, i)

    for step in range(CHUNKS + LAG_PROJECT):
        if step < CHUNKS:
            own(step)
        if 0 <= step - LAG_NEAR < CHUNKS:
            forward_near(step - LAG_NEAR)
        if 0 <= step - LAG_FAR < CHUNKS:
            forward_far(step - LAG_FAR)
        if step >= LAG_PROJECT:
            if step == LAG_PROJECT:
                for copy in loads[10:13]:
                    copy.wait()
            project(step - LAG_PROJECT)

    count = 2 * TENSORS * PAIRS

    def column(at):
        return acc[:, pl.ds(at * HEAD_DIM, HEAD_DIM)]

    def unit(rows_):
        return (
            rows_ * lax.rsqrt(jnp.mean(rows_ * rows_, axis=-1, keepdims=True) + 1e-06)
        ).astype(BF16)

    heads = q_cols // HEAD_DIM
    key = unit(column(heads))
    value = column(heads + 1).astype(BF16)
    mask = (iota((count, count), 0) & 15) == (iota((count, count), 1) & 15)
    pool = jnp.where(
        iota((PAIRS, count), 0) == (iota((PAIRS, count), 1) & 15), 1.0, 0.0
    ).astype(BF16)
    pooled = []
    for head in range(heads):
        query = unit(column(head))
        scores = lax.dot_general(
            query, key, (((1,), (1,)), ((), ())), preferred_element_type=F32
        ) * (SCORE_SCALE / HEAD_DIM)
        expo = jnp.where(mask, jnp.exp(scores), 0.0)
        weights = (expo * (1.0 / jnp.sum(expo, axis=-1, keepdims=True))).astype(BF16)
        context = dot(weights, value).astype(BF16)
        pooled.append(dot(pool, context) * (1.0 / 16.0))
    pooled = jnp.concatenate(pooled, axis=1)
    high = pooled.astype(BF16)
    low = (pooled - high.astype(F32)).astype(BF16)
    both = jnp.concatenate([high, low], axis=0)

    loads[13].wait()
    sums = []

    def partial(dz, core):
        cols = pl.ds(pl.multiple_of((((z + dz) % SIDE) * 2 + core) * share, share), share)
        got = dot(both, out_w[:, cols])
        return got[:PAIRS] + got[PAIRS:] + resid[:, cols]

    def push(source, target_ref, sends, recvs, at, target):
        copy = pltpu.make_async_remote_copy(
            src_ref=source.at[at], dst_ref=target_ref.at[at],
            send_sem=sends.at[at], recv_sem=recvs.at[at],
            device_id=(g, target), device_id_type=MESH,
        )
        copy.start()
        sums.append(copy)
        return copy

    crossing = {}
    for dz in (2, 1, 3, 0):
        across[dz] = partial(dz, 1 - c)
        crossing[dz] = push(across, across_in, tw_s, tw_r, dz, twin)
    coming = []
    for dz in (2, 1, 3, 0):
        mine = partial(dz, c)
        crossing[dz].wait_recv()
        mine = mine + across_in[dz]
        if dz > 0:
            part[dz] = mine.astype(BF16)
            coming.append(push(part, parts_in, rs_s, rs_r, dz, ((z + dz) % SIDE) * 2 + c))
    for copy in coming:
        copy.wait_recv()
    total = mine
    for dz in (1, 2, 3):
        total = total + parts_in[dz].astype(F32)
    live = iota((PAIRS, share), 0) < count_ref[...]
    total = jnp.where(live, total, 0.0)

    stacked = jnp.concatenate([total[:, : share // 2], total[:, share // 2 :]], axis=0)
    got = dot(spread, stacked.astype(BF16))
    fin_out[...] = got.astype(BF16).reshape(GROUPS, 8, share // 2)
    finals = []
    for k in ORDER:
        copy = pltpu.make_async_remote_copy(
            src_ref=fin_out.at[k], dst_ref=fin_in.at[k],
            send_sem=fin_s.at[k], recv_sem=fin_r.at[k],
            device_id=(group_shift(g, k, -1), t), device_id_type=MESH,
        )
        copy.start()
        finals.append(copy)
    load(fin_out.at[0], fin_in.at[0])
    for copies in [idx, sums] + row_copies:
        for copy in copies:
            copy.wait_send()
    for copies in gathers:
        for copy in copies.values():
            copy.wait_send()
    for copy in loads[14:]:
        copy.wait()
    for copy in finals:
        copy.wait()


def owner_sums(wanted_ref, came_ref, lout_ref, rout_ref):
    pick = pick_matrix(wanted_ref[...].reshape(SLOTS, 128))
    span = came_ref.shape[2]
    got = lax.dot_general(
        pick, came_ref[...].reshape(SLOTS, span), (((0,), (0,)), ((), ())),
        preferred_element_type=F32,
    )
    for h in range(2):
        for side, out in enumerate((lout_ref, rout_ref)):
            at = (h * 2 + side) * ROWS
            out[:, pl.ds(h * span, span)] = got[at : at + ROWS]


def on_device(
    left_table, right_table, left_owner, left_row, right_owner, right_row, pair_count,
    norm_gain, query_weight, key_weight, value_weight, output_weight,
):
    width = left_table.shape[2]
    half = width // 2
    share = width // TENSORS
    qkv = query_weight.shape[1] + 2 * key_weight.shape[1]
    vmem = pl.BlockSpec(memory_space=pltpu.VMEM)
    hbm = pl.BlockSpec(memory_space=pl.ANY)
    dma = pltpu.SemaphoreType.DMA
    wanted, came = pl.pallas_call(
        kernel,
        out_shape=(
            jax.ShapeDtypeStruct((GROUPS, 8, 128), F32),
            jax.ShapeDtypeStruct((GROUPS, 8, share // 2), BF16),
        ),
        in_specs=[hbm] * 12,
        out_specs=(hbm, hbm),
        scratch_shapes=[
            pltpu.VMEM((1, PAIRS), jnp.int32),
            pltpu.VMEM((1, PAIRS), jnp.int32),
            pltpu.VMEM((1, PAIRS), jnp.int32),
            pltpu.VMEM((1, PAIRS), jnp.int32),
            pltpu.VMEM((1, 1), jnp.int32),
            pltpu.VMEM((1, width), F32),
            pltpu.VMEM((GROUPS, 8, 128), F32),
            pltpu.VMEM((4 * ROWS, LEAD + half), BF16),
            pltpu.VMEM((width, qkv), BF16),
            pltpu.VMEM(output_weight.shape, BF16),
            pltpu.VMEM((GROUPS, 8, 128), F32),
            pltpu.VMEM((GROUPS, 8, LEAD + half), BF16),
            pltpu.VMEM((GROUPS, 8, LEAD + half), BF16),
            pltpu.VMEM((PAIRS, width), F32),
            pltpu.VMEM((2 * TENSORS * PAIRS, qkv), F32),
            pltpu.VMEM((SIDE, PAIRS, share), F32),
            pltpu.VMEM((SIDE, PAIRS, share), F32),
            pltpu.VMEM((SIDE, PAIRS, share), BF16),
            pltpu.VMEM((SIDE, PAIRS, share), BF16),
            pltpu.VMEM((GROUPS, 8, share // 2), BF16),
            dma((16,)),
            dma((GROUPS,)), dma((GROUPS,)),
            dma((CHUNKS, GROUPS)), dma((CHUNKS, GROUPS)),
            dma((CHUNKS, 8)), dma((CHUNKS, 8)),
            dma((SIDE,)), dma((SIDE,)),
            dma((SIDE,)), dma((SIDE,)),
            dma((GROUPS,)), dma((GROUPS,)),
        ]
        + [pltpu.VMEM((TENSORS, 4 * PAIRS, piece), BF16) for piece in PIECES],
        compiler_params=pltpu.CompilerParams(
            collective_id=0, has_side_effects=True, vmem_limit_bytes=56 * 1024 * 1024
        ),
    )(
        left_owner.reshape(1, PAIRS), left_row.reshape(1, PAIRS),
        right_owner.reshape(1, PAIRS), right_row.reshape(1, PAIRS),
        pair_count.reshape(1, 1), norm_gain.reshape(1, width),
        left_table.reshape(ROWS, width), right_table.reshape(ROWS, width),
        query_weight, key_weight, value_weight, output_weight,
    )
    out = jax.ShapeDtypeStruct((ROWS, share), F32)
    return pl.pallas_call(
        owner_sums, out_shape=(out, out), in_specs=[vmem, vmem], out_specs=(vmem, vmem)
    )(wanted, came)


def solution(mesh):
    return jax.shard_map(
        on_device,
        mesh=mesh,
        in_specs=(
            P("group", "tensor", None), P("group", "tensor", None),
            P("group", None), P("group"), P("group", None), P("group"), P("group"), P(),
            P(None, "tensor"), P(None, "tensor"), P(None, "tensor"), P("tensor", None),
        ),
        out_specs=(P("group", "tensor"), P("group", "tensor")),
        check_vma=False,
    )
```

```python
import jax
import jax.numpy as jnp
from jax import lax
from jax.experimental import pallas as pl
from jax.experimental.pallas import tpu as pltpu
from jax.sharding import PartitionSpec as P

HEAD_DIM = 128
SCORE_SCALE = 4.0
MESH = pl.DeviceIdType.MESH
GROUPS = 16
SIDE = 4
TENSORS = 8
PAIRS = 16
SLOTS = GROUPS * 8
ROWS = 64
PIECES = (1024, 1024, 1024, 1024)
STARTS = tuple(sum(PIECES[:n]) for n in range(len(PIECES)))
CHUNKS = len(PIECES)
LEAD = 128
AHEAD = 4
LAG_NEAR = 1
LAG_FAR = 2
LAG_PROJECT = 3
ORDER = sorted(
    range(1, GROUPS),
    key=lambda k: -(min(k // SIDE, SIDE - k // SIDE) + min(k % SIDE, SIDE - k % SIDE)),
)
F32 = jnp.float32
BF16 = jnp.bfloat16


def iota(shape, axis):
    return lax.broadcasted_iota(jnp.int32, shape, axis)


def group_shift(g, k, sign):
    y, x = g // SIDE, g % SIDE
    ky, kx = k // SIDE, k % SIDE
    return ((y + sign * ky + SIDE) % SIDE) * SIDE + (x + sign * kx + SIDE) % SIDE


def pieces(value):
    high = value.astype(BF16)
    rest = value - high.astype(F32)
    middle = rest.astype(BF16)
    low = (rest - middle.astype(F32)).astype(BF16)
    return high, middle, low


def to_column(row):
    eye = iota((PAIRS, PAIRS), 0) == iota((PAIRS, PAIRS), 1)
    return jnp.sum(jnp.where(eye, row, 0.0), axis=1, keepdims=True)


def slot_keys(owner_row, me):
    owner_col = to_column(owner_row)
    first = iota((PAIRS, PAIRS), 0)
    second = iota((PAIRS, PAIRS), 1)
    same = owner_col == owner_row
    rank_row = jnp.sum(jnp.where(same & (first < second), 1.0, 0.0), axis=0, keepdims=True)
    rank_col = jnp.sum(jnp.where(same & (second < first), 1.0, 0.0), axis=1, keepdims=True)
    want_row = owner_row * 2.0 + rank_row

    def place(owner, rank):
        whole = owner.astype(jnp.int32)
        y, x = me // SIDE, me % SIDE
        ky = (y - (whole >> 2)) & 3
        kx = (x - whole) & 3
        return ((ky * SIDE + kx) * 2).astype(F32) + rank

    return want_row, place(owner_row, rank_row), place(owner_col, rank_col)


def slot_parts(shape, axis):
    at = iota(shape, axis)
    return at >> 3, (at >> 2) & 1, (at >> 1) & 1, at & 1


def requests(want_rows, row_rows, me):
    k, _, side, rank = slot_parts((SLOTS, PAIRS), 0)
    y, x = me // SIDE, me % SIDE
    owner = (((y - (k >> 2)) & 3) << 2) + ((x - k) & 3)
    want = (owner * 2 + rank).astype(F32)
    left = side == 0
    hit = jnp.where(left, want_rows[0], want_rows[1]) == want
    found = jnp.where(hit, jnp.where(left, row_rows[0], row_rows[1]) + 1.0, 0.0)
    return jnp.broadcast_to(jnp.sum(found, axis=1, keepdims=True) - 1.0, (SLOTS, 128))


def pick_matrix(wanted):
    shape = (SLOTS, 4 * ROWS)
    _, half, side, _ = slot_parts(shape, 0)
    lane = iota(shape, 1)
    both = jnp.concatenate([wanted, wanted], axis=1)
    hit = (both == (lane & 63).astype(F32)) & ((lane >> 6) == half * 2 + side)
    return jnp.where(hit, 1.0, 0.0).astype(BF16)


def pack_matrix(place_cols):
    shape = (4 * PAIRS, SLOTS)
    tall = jnp.concatenate(list(place_cols) * 2, axis=0)
    k, half, side, rank = slot_parts(shape, 1)
    hit = (tall == (k * 2 + rank).astype(F32)) & ((iota(shape, 0) >> 4) == half * 2 + side)
    return jnp.where(hit, 1.0, 0.0).astype(BF16)


def spread_matrix(place_rows):
    shape = (SLOTS, 2 * PAIRS)
    k, half, side, rank = slot_parts(shape, 0)
    wide = [jnp.concatenate([row, row], axis=1) for row in place_rows]
    key = (k * 2 + rank).astype(F32)
    hit = (jnp.where(side == 0, wide[0], wide[1]) == key) & ((iota(shape, 1) >> 4) == half)
    return jnp.where(hit, 1.0, 0.0).astype(BF16)


def wait_bytes(ref, sem):
    pltpu.make_async_copy(ref, ref, sem).wait()


def dot(a, b):
    return jnp.dot(a, b, preferred_element_type=F32)


def kernel(
    lo_hbm, lr_hbm, ro_hbm, rr_hbm, count_hbm, gain_hbm,
    lt_ref, rt_ref, wq_ref, wk_ref, wv_ref, wo_ref,
    wanted, fin_in,
    lo_ref, lr_ref, ro_ref, rr_ref, count_ref, gain_ref, inbox,
    table, qkv_w, out_w, outbox, picked, arrived, resid,
    acc, part, parts_in, fin_out,
    load_sem, idx_s, idx_r, row_s, row_r, ag_s, ag_r, rs_s, rs_r,
    fin_s, fin_r, *tokens,
):
    g = lax.axis_index("group")
    t = lax.axis_index("tensor")
    z, c = t // 2, t % 2
    width = out_w.shape[1]
    half = width // 2
    share = width // TENSORS

    barrier = pltpu.get_barrier_semaphore()
    for k in ORDER:
        pl.semaphore_signal(
            barrier, inc=1, device_id=(group_shift(g, k, 1), t), device_id_type=MESH
        )
    for j in range(1, TENSORS):
        pl.semaphore_signal(
            barrier, inc=1, device_id=(g, (t + j) % TENSORS), device_id_type=MESH
        )

    loads = []

    def load(src, dst):
        copy = pltpu.make_async_copy(src, dst, load_sem.at[len(loads)])
        copy.start()
        loads.append(copy)

    for src, dst in (
        (lo_hbm, lo_ref), (lr_hbm, lr_ref), (ro_hbm, ro_ref), (rr_hbm, rr_ref)
    ):
        load(src, dst)
    for h in range(2):
        for side, ref in enumerate((lt_ref, rt_ref)):
            load(
                ref.at[:, pl.ds(h * half, half)],
                table.at[pl.ds((h * 2 + side) * ROWS, ROWS), pl.ds(LEAD, half)],
            )

    q_cols = wq_ref.shape[1]
    kv_cols = wk_ref.shape[1]
    load(gain_hbm, gain_ref)
    load(count_hbm, count_ref)
    load(wq_ref, qkv_w.at[:, pl.ds(0, q_cols)])
    load(wk_ref, qkv_w.at[:, pl.ds(q_cols, kv_cols)])
    load(wv_ref, qkv_w.at[:, pl.ds(q_cols + kv_cols, kv_cols)])
    load(wo_ref, out_w)

    for copy in loads[:4]:
        copy.wait()
    rows = (lr_ref[...].astype(F32), rr_ref[...].astype(F32))
    keys = [slot_keys(ref[...].astype(F32), g) for ref in (lo_ref, ro_ref)]
    asked = requests([key[0] for key in keys], rows, g)
    outbox[...] = asked.reshape(GROUPS, 8, 128)
    pack = pack_matrix([key[2] for key in keys])
    spread = spread_matrix([key[1] for key in keys])

    pl.semaphore_wait(barrier, GROUPS - 1 + TENSORS - 1)

    rest = pl.ds(1, GROUPS - 1)
    for k in ORDER:
        copy = pltpu.make_async_remote_copy(
            src_ref=outbox.at[k], dst_ref=inbox.at[k],
            send_sem=idx_s, recv_sem=idx_r,
            device_id=(group_shift(g, k, -1), t), device_id_type=MESH,
        )
        copy.start()
    inbox[0] = outbox[0]
    for copy in loads[4:10]:
        copy.wait()
    block = half // 8

    def squares(i, sums):
        at = pl.ds(pl.multiple_of(LEAD + i * block, 128), block)
        values = table[:, at].astype(F32)
        values = values * values
        for n in range(block // 128):
            sums = sums + values[:, n * 128 : (n + 1) * 128]
        return sums

    sums = lax.fori_loop(0, 8, squares, jnp.zeros((4 * ROWS, 128), F32))
    sums = jnp.sum(sums[: 2 * ROWS] + sums[2 * ROWS :], axis=1, keepdims=True)
    lane = iota((2 * ROWS, LEAD), 1)
    lead = jnp.zeros((2 * ROWS, LEAD), F32)
    for n, one in enumerate(pieces(lax.rsqrt(sums / width + 1e-05))):
        lead = jnp.where(lane == n, one.astype(F32), lead)
    lead = lead.astype(BF16)
    table[pl.ds(0, 2 * ROWS), pl.ds(0, LEAD)] = lead
    table[pl.ds(2 * ROWS, 2 * ROWS), pl.ds(0, LEAD)] = lead
    wait_bytes(inbox.at[rest], idx_r)
    load(inbox, wanted)

    pick = pick_matrix(inbox[...].reshape(SLOTS, 128))
    def chunk(n):
        return pl.ds(0, LEAD + PIECES[0]) if n == 0 else pl.ds(LEAD + STARTS[n], PIECES[n])

    def ask(n):
        span = chunk(n)
        for k in ORDER:
            copy = pltpu.make_async_remote_copy(
                src_ref=picked.at[k, :, span], dst_ref=arrived.at[k, :, span],
                send_sem=row_s, recv_sem=row_r.at[n],
                device_id=(group_shift(g, k, 1), t), device_id_type=MESH,
            )
            copy.start()

    for n in range(CHUNKS):
        span = chunk(n)
        rows_n = dot(pick, table[:, span])
        picked[:, :, span] = rows_n.astype(BF16).reshape(GROUPS, 8, span.size)
        if n < AHEAD:
            ask(n)
        arrived[0, :, span] = picked[0, :, span]

    up = ((z + 1) % SIDE) * 2 + c
    down = ((z + SIDE - 1) % SIDE) * 2 + c
    far = ((z + 2) % SIDE) * 2 + c
    twin = z * 2 + 1 - c
    def send(n, number, block, side, target):
        place = tokens[n].at[block]
        if side is not None:
            place = place.at[pl.ds(side * 2 * PAIRS, 2 * PAIRS)]
        copy = pltpu.make_async_remote_copy(
            src_ref=place, dst_ref=place,
            send_sem=ag_s.at[n], recv_sem=ag_r.at[n, number],
            device_id=(g, target), device_id_type=MESH,
        )
        copy.start()

    factor = []

    def own(n):
        wait_bytes(arrived.at[rest, :, chunk(n)], row_r.at[n])
        if n + AHEAD < CHUNKS:
            ask(n + AHEAD)
        piece = PIECES[n]
        if n == 0:
            led = dot(pack, arrived[:, :, pl.ds(0, LEAD)].reshape(SLOTS, LEAD))
            led = led[: 2 * PAIRS]
            factor.append(led[:, 0:1] + led[:, 1:2] + led[:, 2:3])
        got = dot(pack, arrived[:, :, pl.ds(LEAD + STARTS[n], piece)].reshape(SLOTS, piece))
        for h in range(2):
            one = got[h * 2 * PAIRS : (h + 1) * 2 * PAIRS]
            cols = pl.ds(h * half + STARTS[n], piece)
            tokens[n][t, pl.ds(h * 2 * PAIRS, 2 * PAIRS), :] = (
                one * factor[0] * gain_ref[:, cols]
            ).astype(BF16)
            resid[:, cols] = (one[:PAIRS] + one[PAIRS:]) * (1.0 / 16.0)
        for number, target in ((0, up), (1, down), (3, twin)):
            send(n, number, t, None, target)

    def forward_near(n):
        wait_bytes(tokens[n].at[down], ag_r.at[n, 0])
        send(n, 2, down, 0, up)
        send(n, 3, down, None, twin)
        wait_bytes(tokens[n].at[up], ag_r.at[n, 1])
        send(n, 2, up, 1, down)
        send(n, 3, up, None, twin)

    def forward_far(n):
        wait_bytes(tokens[n].at[far], ag_r.at[n, 2])
        send(n, 3, far, None, twin)

    def project(n):
        wait_bytes(tokens[n].at[pl.ds(0, SIDE)], ag_r.at[n, 3])
        depth = 512 if PIECES[n] % 512 == 0 else 256

        def block(h, i):
            cols = pl.ds(pl.multiple_of(i * depth, depth), depth)
            a = tokens[n][:, pl.ds(h * 2 * PAIRS, 2 * PAIRS), cols]
            start = pl.multiple_of(h * half + STARTS[n] + i * depth, 256)
            w = qkv_w[pl.ds(start, depth), :]
            return dot(a.reshape(2 * TENSORS * PAIRS, depth), w)

        if n == 0:
            acc[...] = jnp.zeros_like(acc)
        for h in range(2):

            @pl.loop(0, PIECES[n] // depth)
            def _(i):
                acc[...] += block(h, i)

    for step in range(CHUNKS + LAG_PROJECT):
        if step < CHUNKS:
            own(step)
        if 0 <= step - LAG_NEAR < CHUNKS:
            forward_near(step - LAG_NEAR)
        if 0 <= step - LAG_FAR < CHUNKS:
            forward_far(step - LAG_FAR)
        if step >= LAG_PROJECT:
            if step == LAG_PROJECT:
                for copy in loads[10:13]:
                    copy.wait()
            project(step - LAG_PROJECT)

    count = 2 * TENSORS * PAIRS

    def column(at):
        return acc[:, pl.ds(at * HEAD_DIM, HEAD_DIM)]

    def unit(rows_):
        return rows_ * lax.rsqrt(jnp.mean(rows_ * rows_, axis=-1, keepdims=True) + 1e-06)

    heads = q_cols // HEAD_DIM
    block = 8
    rows_b = count // 2

    def blocks(values):
        tiles = values.reshape(rows_b // block, 2, block, HEAD_DIM)
        return [tiles[:, n].reshape(rows_b, HEAD_DIM) for n in range(2)]

    keys_b = blocks(unit(column(heads)))
    values_b = blocks(column(heads + 1))
    mask = (iota((rows_b, rows_b), 0) & 7) == (iota((rows_b, rows_b), 1) & 7)
    pool = jnp.where(
        iota((block, rows_b), 0) == (iota((block, rows_b), 1) & 7), 1.0, 0.0
    ).astype(BF16)
    pooled = []
    for head in range(heads):
        halves = []
        for n, query in enumerate(blocks(unit(column(head)))):
            scores = lax.dot_general(
                query.astype(BF16), keys_b[n].astype(BF16), (((1,), (1,)), ((), ())),
                preferred_element_type=F32,
            ) * (SCORE_SCALE / HEAD_DIM)
            expo = jnp.where(mask, jnp.exp(scores), 0.0)
            weights = (expo * (1.0 / jnp.sum(expo, axis=-1, keepdims=True))).astype(BF16)
            context = dot(weights, values_b[n].astype(BF16)).astype(BF16)
            halves.append(dot(pool, context) * (1.0 / 16.0))
        pooled.append(jnp.concatenate(halves, axis=0))
    pooled = jnp.concatenate(pooled, axis=1)
    high = pooled.astype(BF16)
    low = (pooled - high.astype(F32)).astype(BF16)
    both = jnp.concatenate([high, low], axis=0)

    loads[13].wait()
    for j in (4, 5, 2, 3, 6, 7, 1, 0):
        target = ((z + j // 2) % SIDE) * 2 + (c + j % 2) % 2
        cols = pl.ds(pl.multiple_of(target * share, share), share)
        got = dot(both, out_w[:, cols])
        mine = got[:PAIRS] + got[PAIRS:] + resid[:, cols]
        if j > 0:
            part[j] = mine.astype(BF16)
            copy = pltpu.make_async_remote_copy(
                src_ref=part.at[j], dst_ref=parts_in.at[j],
                send_sem=rs_s, recv_sem=rs_r,
                device_id=(g, target), device_id_type=MESH,
            )
            copy.start()
    others = pl.ds(1, TENSORS - 1)
    wait_bytes(parts_in.at[others], rs_r)
    total = mine
    for j in range(1, TENSORS):
        total = total + parts_in[j].astype(F32)
    live = iota((PAIRS, share), 0) < count_ref[...]
    total = jnp.where(live, total, 0.0)

    stacked = jnp.concatenate([total[:, : share // 2], total[:, share // 2 :]], axis=0)
    got = dot(spread, stacked.astype(BF16))
    fin_out[...] = got.astype(BF16).reshape(GROUPS, 8, share // 2)
    for k in ORDER:
        copy = pltpu.make_async_remote_copy(
            src_ref=fin_out.at[k], dst_ref=fin_in.at[k],
            send_sem=fin_s, recv_sem=fin_r,
            device_id=(group_shift(g, k, -1), t), device_id_type=MESH,
        )
        copy.start()
    load(fin_out.at[0], fin_in.at[0])
    wait_bytes(outbox.at[rest], idx_s)
    wait_bytes(picked.at[rest], row_s)
    for n in range(CHUNKS):
        wait_bytes(tokens[n].at[pl.ds(0, TENSORS - 1)], ag_s.at[n])
    wait_bytes(part.at[others], rs_s)
    for copy in loads[14:]:
        copy.wait()
    wait_bytes(fin_out.at[rest], fin_s)
    wait_bytes(fin_in.at[rest], fin_r)


def owner_sums(wanted_ref, came_ref, lout_ref, rout_ref):
    pick = pick_matrix(wanted_ref[...].reshape(SLOTS, 128))
    span = came_ref.shape[2]
    got = lax.dot_general(
        pick, came_ref[...].reshape(SLOTS, span), (((0,), (0,)), ((), ())),
        preferred_element_type=F32,
    )
    for h in range(2):
        for side, out in enumerate((lout_ref, rout_ref)):
            at = (h * 2 + side) * ROWS
            out[:, pl.ds(h * span, span)] = got[at : at + ROWS]


def on_device(
    left_table, right_table, left_owner, left_row, right_owner, right_row, pair_count,
    norm_gain, query_weight, key_weight, value_weight, output_weight,
):
    width = left_table.shape[2]
    half = width // 2
    share = width // TENSORS
    qkv = query_weight.shape[1] + 2 * key_weight.shape[1]
    vmem = pl.BlockSpec(memory_space=pltpu.VMEM)
    hbm = pl.BlockSpec(memory_space=pl.ANY)
    dma = pltpu.SemaphoreType.DMA
    wanted, came = pl.pallas_call(
        kernel,
        out_shape=(
            jax.ShapeDtypeStruct((GROUPS, 8, 128), F32),
            jax.ShapeDtypeStruct((GROUPS, 8, share // 2), BF16),
        ),
        in_specs=[hbm] * 12,
        out_specs=(hbm, hbm),
        scratch_shapes=[
            pltpu.VMEM((1, PAIRS), jnp.int32),
            pltpu.VMEM((1, PAIRS), jnp.int32),
            pltpu.VMEM((1, PAIRS), jnp.int32),
            pltpu.VMEM((1, PAIRS), jnp.int32),
            pltpu.VMEM((1, 1), jnp.int32),
            pltpu.VMEM((1, width), F32),
            pltpu.VMEM((GROUPS, 8, 128), F32),
            pltpu.VMEM((4 * ROWS, LEAD + half), BF16),
            pltpu.VMEM((width, qkv), BF16),
            pltpu.VMEM(output_weight.shape, BF16),
            pltpu.VMEM((GROUPS, 8, 128), F32),
            pltpu.VMEM((GROUPS, 8, LEAD + half), BF16),
            pltpu.VMEM((GROUPS, 8, LEAD + half), BF16),
            pltpu.VMEM((PAIRS, width), F32),
            pltpu.VMEM((2 * TENSORS * PAIRS, qkv), F32),
            pltpu.VMEM((TENSORS, PAIRS, share), BF16),
            pltpu.VMEM((TENSORS, PAIRS, share), BF16),
            pltpu.VMEM((GROUPS, 8, share // 2), BF16),
            dma((16,)),
            dma, dma,
            dma, dma((CHUNKS,)),
            dma((CHUNKS,)), dma((CHUNKS, SIDE)),
            dma, dma,
            dma, dma,
        ]
        + [pltpu.VMEM((TENSORS, 4 * PAIRS, piece), BF16) for piece in PIECES],
        compiler_params=pltpu.CompilerParams(
            collective_id=0, has_side_effects=True, vmem_limit_bytes=56 * 1024 * 1024
        ),
    )(
        left_owner.reshape(1, PAIRS), left_row.reshape(1, PAIRS),
        right_owner.reshape(1, PAIRS), right_row.reshape(1, PAIRS),
        pair_count.reshape(1, 1), norm_gain.reshape(1, width),
        left_table.reshape(ROWS, width), right_table.reshape(ROWS, width),
        query_weight, key_weight, value_weight, output_weight,
    )
    out = jax.ShapeDtypeStruct((ROWS, share), F32)
    return pl.pallas_call(
        owner_sums, out_shape=(out, out), in_specs=[vmem, vmem], out_specs=(vmem, vmem)
    )(wanted, came)


def solution(mesh):
    return jax.shard_map(
        on_device,
        mesh=mesh,
        in_specs=(
            P("group", "tensor", None), P("group", "tensor", None),
            P("group", None), P("group"), P("group", None), P("group"), P("group"), P(),
            P(None, "tensor"), P(None, "tensor"), P(None, "tensor"), P("tensor", None),
        ),
        out_specs=(P("group", "tensor"), P("group", "tensor")),
        check_vma=False,
    )
```

```python
import jax
import jax.numpy as jnp
from jax import lax
from jax.experimental import pallas as pl
from jax.experimental.pallas import tpu as pltpu
from jax.sharding import PartitionSpec as P

HEAD_DIM = 128
SCORE_SCALE = 4.0
MESH = pl.DeviceIdType.MESH
GROUPS = 16
SIDE = 4
TENSORS = 8
PAIRS = 16
SLOTS = GROUPS * 8
ROWS = 64
PIECES = (1024, 1024, 1024, 1024)
STARTS = tuple(sum(PIECES[:n]) for n in range(len(PIECES)))
CHUNKS = len(PIECES)
LEAD = 128
AHEAD = 3
ORDER = sorted(
    range(1, GROUPS),
    key=lambda k: -(min(k // SIDE, SIDE - k // SIDE) + min(k % SIDE, SIDE - k % SIDE)),
)
F32 = jnp.float32
BF16 = jnp.bfloat16


def iota(shape, axis):
    return lax.broadcasted_iota(jnp.int32, shape, axis)


def group_shift(g, k, sign):
    y, x = g // SIDE, g % SIDE
    ky, kx = k // SIDE, k % SIDE
    return ((y + sign * ky + SIDE) % SIDE) * SIDE + (x + sign * kx + SIDE) % SIDE


def pieces(value):
    high = value.astype(BF16)
    rest = value - high.astype(F32)
    middle = rest.astype(BF16)
    low = (rest - middle.astype(F32)).astype(BF16)
    return high, middle, low


def to_column(row):
    eye = iota((PAIRS, PAIRS), 0) == iota((PAIRS, PAIRS), 1)
    return jnp.sum(jnp.where(eye, row, 0.0), axis=1, keepdims=True)


def slot_keys(owner_row, me):
    owner_col = to_column(owner_row)
    first = iota((PAIRS, PAIRS), 0)
    second = iota((PAIRS, PAIRS), 1)
    same = owner_col == owner_row
    rank_row = jnp.sum(jnp.where(same & (first < second), 1.0, 0.0), axis=0, keepdims=True)
    rank_col = jnp.sum(jnp.where(same & (second < first), 1.0, 0.0), axis=1, keepdims=True)
    want_row = owner_row * 2.0 + rank_row

    def place(owner, rank):
        whole = owner.astype(jnp.int32)
        y, x = me // SIDE, me % SIDE
        ky = (y - (whole >> 2)) & 3
        kx = (x - whole) & 3
        return ((ky * SIDE + kx) * 2).astype(F32) + rank

    return want_row, place(owner_row, rank_row), place(owner_col, rank_col)


def slot_parts(shape, axis):
    at = iota(shape, axis)
    return at >> 3, (at >> 2) & 1, (at >> 1) & 1, at & 1


def requests(want_rows, row_rows, me):
    k, _, side, rank = slot_parts((SLOTS, PAIRS), 0)
    y, x = me // SIDE, me % SIDE
    owner = (((y - (k >> 2)) & 3) << 2) + ((x - k) & 3)
    want = (owner * 2 + rank).astype(F32)
    left = side == 0
    hit = jnp.where(left, want_rows[0], want_rows[1]) == want
    found = jnp.where(hit, jnp.where(left, row_rows[0], row_rows[1]) + 1.0, 0.0)
    return jnp.broadcast_to(jnp.sum(found, axis=1, keepdims=True) - 1.0, (SLOTS, 128))


def pick_matrix(wanted):
    shape = (SLOTS, 4 * ROWS)
    _, half, side, _ = slot_parts(shape, 0)
    lane = iota(shape, 1)
    both = jnp.concatenate([wanted, wanted], axis=1)
    hit = (both == (lane & 63).astype(F32)) & ((lane >> 6) == half * 2 + side)
    return jnp.where(hit, 1.0, 0.0).astype(BF16)


def pack_matrix(place_cols):
    shape = (4 * PAIRS, SLOTS)
    tall = jnp.concatenate(list(place_cols) * 2, axis=0)
    k, half, side, rank = slot_parts(shape, 1)
    hit = (tall == (k * 2 + rank).astype(F32)) & ((iota(shape, 0) >> 4) == half * 2 + side)
    return jnp.where(hit, 1.0, 0.0).astype(BF16)


def spread_matrix(place_rows):
    shape = (SLOTS, 2 * PAIRS)
    k, half, side, rank = slot_parts(shape, 0)
    wide = [jnp.concatenate([row, row], axis=1) for row in place_rows]
    key = (k * 2 + rank).astype(F32)
    hit = (jnp.where(side == 0, wide[0], wide[1]) == key) & ((iota(shape, 1) >> 4) == half)
    return jnp.where(hit, 1.0, 0.0).astype(BF16)


def wait_bytes(ref, sem):
    pltpu.make_async_copy(ref, ref, sem).wait()


def dot(a, b):
    return jnp.dot(a, b, preferred_element_type=F32)


def kernel(
    lo_hbm, lr_hbm, ro_hbm, rr_hbm, count_hbm, gain_hbm,
    lt_ref, rt_ref, wq_ref, wk_ref, wv_ref, wo_ref,
    wanted, fin_in,
    lo_ref, lr_ref, ro_ref, rr_ref, count_ref, gain_ref, inbox,
    table, qkv_w, out_w, outbox, picked, arrived, resid,
    acc, part, parts_in, fin_out,
    load_sem, idx_s, idx_r, row_s, row_r, ag_s, ag_r, rs_s, rs_r,
    fin_s, fin_r, *tokens,
):
    g = lax.axis_index("group")
    t = lax.axis_index("tensor")
    z, c = t // 2, t % 2
    width = out_w.shape[1]
    half = width // 2
    share = width // TENSORS

    barrier = pltpu.get_barrier_semaphore()
    for k in ORDER:
        pl.semaphore_signal(
            barrier, inc=1, device_id=(group_shift(g, k, 1), t), device_id_type=MESH
        )
    for j in range(1, TENSORS):
        pl.semaphore_signal(
            barrier, inc=1, device_id=(g, (t + j) % TENSORS), device_id_type=MESH
        )

    loads = []

    def load(src, dst):
        copy = pltpu.make_async_copy(src, dst, load_sem.at[len(loads)])
        copy.start()
        loads.append(copy)

    for src, dst in (
        (lo_hbm, lo_ref), (lr_hbm, lr_ref), (ro_hbm, ro_ref), (rr_hbm, rr_ref)
    ):
        load(src, dst)
    for h in range(2):
        for side, ref in enumerate((lt_ref, rt_ref)):
            load(
                ref.at[:, pl.ds(h * half, half)],
                table.at[pl.ds((h * 2 + side) * ROWS, ROWS), pl.ds(LEAD, half)],
            )

    q_cols = wq_ref.shape[1]
    kv_cols = wk_ref.shape[1]
    load(gain_hbm, gain_ref)
    load(count_hbm, count_ref)
    load(wq_ref, qkv_w.at[:, pl.ds(0, q_cols)])
    load(wk_ref, qkv_w.at[:, pl.ds(q_cols, kv_cols)])
    load(wv_ref, qkv_w.at[:, pl.ds(q_cols + kv_cols, kv_cols)])
    load(wo_ref, out_w)

    for copy in loads[:4]:
        copy.wait()
    rows = (lr_ref[...].astype(F32), rr_ref[...].astype(F32))
    keys = [slot_keys(ref[...].astype(F32), g) for ref in (lo_ref, ro_ref)]
    asked = requests([key[0] for key in keys], rows, g)
    outbox[...] = asked.reshape(GROUPS, 8, 128)
    pack = pack_matrix([key[2] for key in keys])
    spread = spread_matrix([key[1] for key in keys])

    pl.semaphore_wait(barrier, GROUPS - 1 + TENSORS - 1)

    rest = pl.ds(1, GROUPS - 1)
    for k in ORDER:
        copy = pltpu.make_async_remote_copy(
            src_ref=outbox.at[k], dst_ref=inbox.at[k],
            send_sem=idx_s, recv_sem=idx_r,
            device_id=(group_shift(g, k, -1), t), device_id_type=MESH,
        )
        copy.start()
    inbox[0] = outbox[0]
    for copy in loads[4:10]:
        copy.wait()
    block = half // 8

    def squares(i, sums):
        at = pl.ds(pl.multiple_of(LEAD + i * block, 128), block)
        values = table[:, at].astype(F32)
        values = values * values
        for n in range(block // 128):
            sums = sums + values[:, n * 128 : (n + 1) * 128]
        return sums

    sums = lax.fori_loop(0, 8, squares, jnp.zeros((4 * ROWS, 128), F32))
    sums = jnp.sum(sums[: 2 * ROWS] + sums[2 * ROWS :], axis=1, keepdims=True)
    lane = iota((2 * ROWS, LEAD), 1)
    lead = jnp.zeros((2 * ROWS, LEAD), F32)
    for n, one in enumerate(pieces(lax.rsqrt(sums / width + 1e-05))):
        lead = jnp.where(lane == n, one.astype(F32), lead)
    lead = lead.astype(BF16)
    table[pl.ds(0, 2 * ROWS), pl.ds(0, LEAD)] = lead
    table[pl.ds(2 * ROWS, 2 * ROWS), pl.ds(0, LEAD)] = lead
    wait_bytes(inbox.at[rest], idx_r)
    load(inbox, wanted)

    pick = pick_matrix(inbox[...].reshape(SLOTS, 128))
    def chunk(n):
        return pl.ds(0, LEAD + PIECES[0]) if n == 0 else pl.ds(LEAD + STARTS[n], PIECES[n])

    def ask(n):
        span = chunk(n)
        for k in ORDER:
            copy = pltpu.make_async_remote_copy(
                src_ref=picked.at[k, :, span], dst_ref=arrived.at[k, :, span],
                send_sem=row_s, recv_sem=row_r.at[n],
                device_id=(group_shift(g, k, 1), t), device_id_type=MESH,
            )
            copy.start()

    for n in range(CHUNKS):
        span = chunk(n)
        rows_n = dot(pick, table[:, span])
        picked[:, :, span] = rows_n.astype(BF16).reshape(GROUPS, 8, span.size)
        if n < AHEAD:
            ask(n)
        arrived[0, :, span] = picked[0, :, span]

    up = ((z + 1) % SIDE) * 2 + c
    down = ((z + SIDE - 1) % SIDE) * 2 + c
    far = ((z + 2) % SIDE) * 2 + c
    twin = z * 2 + 1 - c
    def send(n, number, block, side, target):
        place = tokens[n].at[block]
        if side is not None:
            place = place.at[pl.ds(side * 2 * PAIRS, 2 * PAIRS)]
        copy = pltpu.make_async_remote_copy(
            src_ref=place, dst_ref=place,
            send_sem=ag_s.at[n], recv_sem=ag_r.at[n, number],
            device_id=(g, target), device_id_type=MESH,
        )
        copy.start()

    factor = []

    def own(n):
        wait_bytes(arrived.at[rest, :, chunk(n)], row_r.at[n])
        if n + AHEAD < CHUNKS:
            ask(n + AHEAD)
        piece = PIECES[n]
        if n == 0:
            led = dot(pack, arrived[:, :, pl.ds(0, LEAD)].reshape(SLOTS, LEAD))
            led = led[: 2 * PAIRS]
            factor.append(led[:, 0:1] + led[:, 1:2] + led[:, 2:3])
        got = dot(pack, arrived[:, :, pl.ds(LEAD + STARTS[n], piece)].reshape(SLOTS, piece))
        for h in range(2):
            one = got[h * 2 * PAIRS : (h + 1) * 2 * PAIRS]
            cols = pl.ds(h * half + STARTS[n], piece)
            tokens[n][t, pl.ds(h * 2 * PAIRS, 2 * PAIRS), :] = (
                one * factor[0] * gain_ref[:, cols]
            ).astype(BF16)
            resid[:, cols] = (one[:PAIRS] + one[PAIRS:]) * (1.0 / 16.0)
        for number, target in ((0, up), (1, down), (3, twin)):
            send(n, number, t, None, target)

    def forward_near(n):
        wait_bytes(tokens[n].at[down], ag_r.at[n, 0])
        send(n, 2, down, 0, up)
        send(n, 3, down, None, twin)
        wait_bytes(tokens[n].at[up], ag_r.at[n, 1])
        send(n, 2, up, 1, down)
        send(n, 3, up, None, twin)

    def forward_far(n):
        wait_bytes(tokens[n].at[far], ag_r.at[n, 2])
        send(n, 3, far, None, twin)

    def project(n):
        wait_bytes(tokens[n].at[pl.ds(0, SIDE)], ag_r.at[n, 3])
        depth = 512 if PIECES[n] % 512 == 0 else 256

        def block(h, i):
            cols = pl.ds(pl.multiple_of(i * depth, depth), depth)
            a = tokens[n][:, pl.ds(h * 2 * PAIRS, 2 * PAIRS), cols]
            start = pl.multiple_of(h * half + STARTS[n] + i * depth, 256)
            w = qkv_w[pl.ds(start, depth), :]
            return dot(a.reshape(2 * TENSORS * PAIRS, depth), w)

        if n == 0:
            acc[...] = jnp.zeros_like(acc)
        for h in range(2):

            @pl.loop(0, PIECES[n] // depth)
            def _(i):
                acc[...] += block(h, i)

    steps = (
        (own, 0), (own, 1), (forward_near, 0), (own, 2),
        (forward_near, 1), (own, 3), (forward_far, 0), (forward_near, 2),
        (project, 0), (forward_far, 1), (forward_near, 3), (forward_far, 2),
        (project, 1), (forward_far, 3), (project, 2), (project, 3),
    )
    for step, n in steps:
        if step is project and n == 0:
            for copy in loads[10:13]:
                copy.wait()
        step(n)

    count = 2 * TENSORS * PAIRS

    def column(at):
        return acc[:, pl.ds(at * HEAD_DIM, HEAD_DIM)]

    def unit(rows_):
        return rows_ * lax.rsqrt(jnp.mean(rows_ * rows_, axis=-1, keepdims=True) + 1e-06)

    heads = q_cols // HEAD_DIM
    block = 8
    rows_b = count // 2

    def blocks(values):
        tiles = values.reshape(rows_b // block, 2, block, HEAD_DIM)
        return [tiles[:, n].reshape(rows_b, HEAD_DIM) for n in range(2)]

    keys_b = blocks(unit(column(heads)))
    values_b = blocks(column(heads + 1))
    mask = (iota((rows_b, rows_b), 0) & 7) == (iota((rows_b, rows_b), 1) & 7)
    pool = jnp.where(
        iota((block, rows_b), 0) == (iota((block, rows_b), 1) & 7), 1.0, 0.0
    ).astype(BF16)
    pooled = []
    for head in range(heads):
        halves = []
        for n, query in enumerate(blocks(unit(column(head)))):
            scores = lax.dot_general(
                query.astype(BF16), keys_b[n].astype(BF16), (((1,), (1,)), ((), ())),
                preferred_element_type=F32,
            ) * (SCORE_SCALE / HEAD_DIM)
            expo = jnp.where(mask, jnp.exp(scores), 0.0)
            weights = (expo * (1.0 / jnp.sum(expo, axis=-1, keepdims=True))).astype(BF16)
            context = dot(weights, values_b[n].astype(BF16)).astype(BF16)
            halves.append(dot(pool, context) * (1.0 / 16.0))
        pooled.append(jnp.concatenate(halves, axis=0))
    pooled = jnp.concatenate(pooled, axis=1)
    high = pooled.astype(BF16)
    low = (pooled - high.astype(F32)).astype(BF16)
    both = jnp.concatenate([high, low], axis=0)

    loads[13].wait()
    for j in (4, 5, 2, 3, 6, 7, 1, 0):
        target = ((z + j // 2) % SIDE) * 2 + (c + j % 2) % 2
        cols = pl.ds(pl.multiple_of(target * share, share), share)
        got = dot(both, out_w[:, cols])
        mine = got[:PAIRS] + got[PAIRS:] + resid[:, cols]
        if j > 0:
            part[j] = mine.astype(BF16)
            copy = pltpu.make_async_remote_copy(
                src_ref=part.at[j], dst_ref=parts_in.at[j],
                send_sem=rs_s, recv_sem=rs_r,
                device_id=(g, target), device_id_type=MESH,
            )
            copy.start()
    others = pl.ds(1, TENSORS - 1)
    wait_bytes(parts_in.at[others], rs_r)
    total = mine
    for j in range(1, TENSORS):
        total = total + parts_in[j].astype(F32)
    live = iota((PAIRS, share), 0) < count_ref[...]
    total = jnp.where(live, total, 0.0)

    stacked = jnp.concatenate([total[:, : share // 2], total[:, share // 2 :]], axis=0)
    got = dot(spread, stacked.astype(BF16))
    fin_out[...] = got.astype(BF16).reshape(GROUPS, 8, share // 2)
    for k in ORDER:
        copy = pltpu.make_async_remote_copy(
            src_ref=fin_out.at[k], dst_ref=fin_in.at[k],
            send_sem=fin_s, recv_sem=fin_r,
            device_id=(group_shift(g, k, -1), t), device_id_type=MESH,
        )
        copy.start()
    load(fin_out.at[0], fin_in.at[0])
    wait_bytes(outbox.at[rest], idx_s)
    wait_bytes(picked.at[rest], row_s)
    for n in range(CHUNKS):
        wait_bytes(tokens[n].at[pl.ds(0, TENSORS - 1)], ag_s.at[n])
    wait_bytes(part.at[others], rs_s)
    for copy in loads[14:]:
        copy.wait()
    wait_bytes(fin_out.at[rest], fin_s)
    wait_bytes(fin_in.at[rest], fin_r)


def owner_sums(wanted_ref, came_ref, lout_ref, rout_ref):
    pick = pick_matrix(wanted_ref[...].reshape(SLOTS, 128))
    span = came_ref.shape[2]
    got = lax.dot_general(
        pick, came_ref[...].reshape(SLOTS, span), (((0,), (0,)), ((), ())),
        preferred_element_type=F32,
    )
    for h in range(2):
        for side, out in enumerate((lout_ref, rout_ref)):
            at = (h * 2 + side) * ROWS
            out[:, pl.ds(h * span, span)] = got[at : at + ROWS]


def on_device(
    left_table, right_table, left_owner, left_row, right_owner, right_row, pair_count,
    norm_gain, query_weight, key_weight, value_weight, output_weight,
):
    width = left_table.shape[2]
    half = width // 2
    share = width // TENSORS
    qkv = query_weight.shape[1] + 2 * key_weight.shape[1]
    vmem = pl.BlockSpec(memory_space=pltpu.VMEM)
    hbm = pl.BlockSpec(memory_space=pl.ANY)
    dma = pltpu.SemaphoreType.DMA
    wanted, came = pl.pallas_call(
        kernel,
        out_shape=(
            jax.ShapeDtypeStruct((GROUPS, 8, 128), F32),
            jax.ShapeDtypeStruct((GROUPS, 8, share // 2), BF16),
        ),
        in_specs=[hbm] * 12,
        out_specs=(hbm, hbm),
        scratch_shapes=[
            pltpu.VMEM((1, PAIRS), jnp.int32),
            pltpu.VMEM((1, PAIRS), jnp.int32),
            pltpu.VMEM((1, PAIRS), jnp.int32),
            pltpu.VMEM((1, PAIRS), jnp.int32),
            pltpu.VMEM((1, 1), jnp.int32),
            pltpu.VMEM((1, width), F32),
            pltpu.VMEM((GROUPS, 8, 128), F32),
            pltpu.VMEM((4 * ROWS, LEAD + half), BF16),
            pltpu.VMEM((width, qkv), BF16),
            pltpu.VMEM(output_weight.shape, BF16),
            pltpu.VMEM((GROUPS, 8, 128), F32),
            pltpu.VMEM((GROUPS, 8, LEAD + half), BF16),
            pltpu.VMEM((GROUPS, 8, LEAD + half), BF16),
            pltpu.VMEM((PAIRS, width), F32),
            pltpu.VMEM((2 * TENSORS * PAIRS, qkv), F32),
            pltpu.VMEM((TENSORS, PAIRS, share), BF16),
            pltpu.VMEM((TENSORS, PAIRS, share), BF16),
            pltpu.VMEM((GROUPS, 8, share // 2), BF16),
            dma((16,)),
            dma, dma,
            dma, dma((CHUNKS,)),
            dma((CHUNKS,)), dma((CHUNKS, SIDE)),
            dma, dma,
            dma, dma,
        ]
        + [pltpu.VMEM((TENSORS, 4 * PAIRS, piece), BF16) for piece in PIECES],
        compiler_params=pltpu.CompilerParams(
            collective_id=0, has_side_effects=True, vmem_limit_bytes=56 * 1024 * 1024
        ),
    )(
        left_owner.reshape(1, PAIRS), left_row.reshape(1, PAIRS),
        right_owner.reshape(1, PAIRS), right_row.reshape(1, PAIRS),
        pair_count.reshape(1, 1), norm_gain.reshape(1, width),
        left_table.reshape(ROWS, width), right_table.reshape(ROWS, width),
        query_weight, key_weight, value_weight, output_weight,
    )
    out = jax.ShapeDtypeStruct((ROWS, share), F32)
    return pl.pallas_call(
        owner_sums, out_shape=(out, out), in_specs=[vmem, vmem], out_specs=(vmem, vmem)
    )(wanted, came)


def solution(mesh):
    return jax.shard_map(
        on_device,
        mesh=mesh,
        in_specs=(
            P("group", "tensor", None), P("group", "tensor", None),
            P("group", None), P("group"), P("group", None), P("group"), P("group"), P(),
            P(None, "tensor"), P(None, "tensor"), P(None, "tensor"), P("tensor", None),
        ),
        out_specs=(P("group", "tensor"), P("group", "tensor")),
        check_vma=False,
    )
```

```python
import jax
import jax.numpy as jnp
from jax import lax
from jax.experimental import pallas as pl
from jax.experimental.pallas import tpu as pltpu
from jax.sharding import PartitionSpec as P

HEAD_DIM = 128
SCORE_SCALE = 4.0
MESH = pl.DeviceIdType.MESH
GROUPS = 16
SIDE = 4
TENSORS = 8
PAIRS = 16
SLOTS = GROUPS * 8
ROWS = 64
PIECES = (1024, 1024, 1024, 1024)
STARTS = tuple(sum(PIECES[:n]) for n in range(len(PIECES)))
CHUNKS = len(PIECES)
LEAD = 128
AHEAD = 3
ORDER = sorted(
    range(1, GROUPS),
    key=lambda k: -(min(k // SIDE, SIDE - k // SIDE) + min(k % SIDE, SIDE - k % SIDE)),
)
F32 = jnp.float32
BF16 = jnp.bfloat16


def iota(shape, axis):
    return lax.broadcasted_iota(jnp.int32, shape, axis)


def group_shift(g, k, sign):
    y, x = g // SIDE, g % SIDE
    ky, kx = k // SIDE, k % SIDE
    return ((y + sign * ky + SIDE) % SIDE) * SIDE + (x + sign * kx + SIDE) % SIDE


def pieces(value):
    high = value.astype(BF16)
    rest = value - high.astype(F32)
    middle = rest.astype(BF16)
    low = (rest - middle.astype(F32)).astype(BF16)
    return high, middle, low


def to_column(row):
    eye = iota((PAIRS, PAIRS), 0) == iota((PAIRS, PAIRS), 1)
    return jnp.sum(jnp.where(eye, row, 0.0), axis=1, keepdims=True)


def slot_keys(owner_row, me):
    owner_col = to_column(owner_row)
    first = iota((PAIRS, PAIRS), 0)
    second = iota((PAIRS, PAIRS), 1)
    same = owner_col == owner_row
    rank_row = jnp.sum(jnp.where(same & (first < second), 1.0, 0.0), axis=0, keepdims=True)
    rank_col = jnp.sum(jnp.where(same & (second < first), 1.0, 0.0), axis=1, keepdims=True)
    want_row = owner_row * 2.0 + rank_row

    def place(owner, rank):
        whole = owner.astype(jnp.int32)
        y, x = me // SIDE, me % SIDE
        ky = (y - (whole >> 2)) & 3
        kx = (x - whole) & 3
        return ((ky * SIDE + kx) * 2).astype(F32) + rank

    return want_row, place(owner_row, rank_row), place(owner_col, rank_col)


def slot_parts(shape, axis):
    at = iota(shape, axis)
    return at >> 3, (at >> 2) & 1, (at >> 1) & 1, at & 1


def requests(want_rows, row_rows, me):
    k, _, side, rank = slot_parts((SLOTS, PAIRS), 0)
    y, x = me // SIDE, me % SIDE
    owner = (((y - (k >> 2)) & 3) << 2) + ((x - k) & 3)
    want = (owner * 2 + rank).astype(F32)
    left = side == 0
    hit = jnp.where(left, want_rows[0], want_rows[1]) == want
    found = jnp.where(hit, jnp.where(left, row_rows[0], row_rows[1]) + 1.0, 0.0)
    return jnp.broadcast_to(jnp.sum(found, axis=1, keepdims=True) - 1.0, (SLOTS, 128))


def pick_matrix(wanted):
    shape = (SLOTS, 4 * ROWS)
    _, half, side, _ = slot_parts(shape, 0)
    lane = iota(shape, 1)
    both = jnp.concatenate([wanted, wanted], axis=1)
    hit = (both == (lane & 63).astype(F32)) & ((lane >> 6) == half * 2 + side)
    return jnp.where(hit, 1.0, 0.0).astype(BF16)


def pack_matrix(place_cols):
    shape = (4 * PAIRS, SLOTS)
    tall = jnp.concatenate(list(place_cols) * 2, axis=0)
    k, half, side, rank = slot_parts(shape, 1)
    hit = (tall == (k * 2 + rank).astype(F32)) & ((iota(shape, 0) >> 4) == half * 2 + side)
    return jnp.where(hit, 1.0, 0.0).astype(BF16)


def spread_matrix(place_rows):
    shape = (SLOTS, 2 * PAIRS)
    k, half, side, rank = slot_parts(shape, 0)
    wide = [jnp.concatenate([row, row], axis=1) for row in place_rows]
    key = (k * 2 + rank).astype(F32)
    hit = (jnp.where(side == 0, wide[0], wide[1]) == key) & ((iota(shape, 1) >> 4) == half)
    return jnp.where(hit, 1.0, 0.0).astype(BF16)


def wait_bytes(ref, sem):
    pltpu.make_async_copy(ref, ref, sem).wait()


def dot(a, b):
    return jnp.dot(a, b, preferred_element_type=F32)


def kernel(
    lo_hbm, lr_hbm, ro_hbm, rr_hbm, count_hbm, gain_hbm,
    lt_ref, rt_ref, wq_ref, wk_ref, wv_ref, wo_ref,
    wanted, fin_in,
    lo_ref, lr_ref, ro_ref, rr_ref, count_ref, gain_ref, inbox,
    table, qkv_w, out_w, outbox, picked, arrived, resid,
    acc, part, parts_in, fin_out,
    load_sem, idx_s, idx_r, row_s, row_r, ag_s, ag_r, rs_s, rs_r,
    fin_s, fin_r, *tokens,
):
    g = lax.axis_index("group")
    t = lax.axis_index("tensor")
    z, c = t // 2, t % 2
    width = out_w.shape[1]
    half = width // 2
    share = width // TENSORS

    barrier = pltpu.get_barrier_semaphore()
    for k in ORDER:
        pl.semaphore_signal(
            barrier, inc=1, device_id=(group_shift(g, k, 1), t), device_id_type=MESH
        )
    for j in range(1, TENSORS):
        pl.semaphore_signal(
            barrier, inc=1, device_id=(g, (t + j) % TENSORS), device_id_type=MESH
        )

    loads = []

    def load(src, dst):
        copy = pltpu.make_async_copy(src, dst, load_sem.at[len(loads)])
        copy.start()
        loads.append(copy)

    for src, dst in (
        (lo_hbm, lo_ref), (lr_hbm, lr_ref), (ro_hbm, ro_ref), (rr_hbm, rr_ref)
    ):
        load(src, dst)
    for h in range(2):
        for side, ref in enumerate((lt_ref, rt_ref)):
            load(
                ref.at[:, pl.ds(h * half, half)],
                table.at[pl.ds((h * 2 + side) * ROWS, ROWS), pl.ds(LEAD, half)],
            )

    q_cols = wq_ref.shape[1]
    kv_cols = wk_ref.shape[1]
    load(gain_hbm, gain_ref)
    load(count_hbm, count_ref)
    load(wq_ref, qkv_w.at[:, pl.ds(0, q_cols)])
    load(wk_ref, qkv_w.at[:, pl.ds(q_cols, kv_cols)])
    load(wv_ref, qkv_w.at[:, pl.ds(q_cols + kv_cols, kv_cols)])
    load(wo_ref, out_w)

    for copy in loads[:4]:
        copy.wait()
    rows = (lr_ref[...].astype(F32), rr_ref[...].astype(F32))
    keys = [slot_keys(ref[...].astype(F32), g) for ref in (lo_ref, ro_ref)]
    asked = requests([key[0] for key in keys], rows, g)
    outbox[...] = asked.reshape(GROUPS, 8, 128)
    pack = pack_matrix([key[2] for key in keys])
    spread = spread_matrix([key[1] for key in keys])

    pl.semaphore_wait(barrier, GROUPS - 1 + TENSORS - 1)

    rest = pl.ds(1, GROUPS - 1)
    for k in ORDER:
        copy = pltpu.make_async_remote_copy(
            src_ref=outbox.at[k], dst_ref=inbox.at[k],
            send_sem=idx_s, recv_sem=idx_r,
            device_id=(group_shift(g, k, -1), t), device_id_type=MESH,
        )
        copy.start()
    inbox[0] = outbox[0]
    for copy in loads[4:10]:
        copy.wait()
    block = half // 8

    def squares(i, sums):
        at = pl.ds(pl.multiple_of(LEAD + i * block, 128), block)
        values = table[:, at].astype(F32)
        values = values * values
        for n in range(block // 128):
            sums = sums + values[:, n * 128 : (n + 1) * 128]
        return sums

    sums = lax.fori_loop(0, 8, squares, jnp.zeros((4 * ROWS, 128), F32))
    sums = jnp.sum(sums[: 2 * ROWS] + sums[2 * ROWS :], axis=1, keepdims=True)
    lane = iota((2 * ROWS, LEAD), 1)
    lead = jnp.zeros((2 * ROWS, LEAD), F32)
    for n, one in enumerate(pieces(lax.rsqrt(sums / width + 1e-05))):
        lead = jnp.where(lane == n, one.astype(F32), lead)
    lead = lead.astype(BF16)
    table[pl.ds(0, 2 * ROWS), pl.ds(0, LEAD)] = lead
    table[pl.ds(2 * ROWS, 2 * ROWS), pl.ds(0, LEAD)] = lead
    wait_bytes(inbox.at[rest], idx_r)
    load(inbox, wanted)

    pick = pick_matrix(inbox[...].reshape(SLOTS, 128))
    def chunk(n):
        return pl.ds(0, LEAD + PIECES[0]) if n == 0 else pl.ds(LEAD + STARTS[n], PIECES[n])

    def ask(n):
        span = chunk(n)
        for k in ORDER:
            copy = pltpu.make_async_remote_copy(
                src_ref=picked.at[k, :, span], dst_ref=arrived.at[k, :, span],
                send_sem=row_s, recv_sem=row_r.at[n],
                device_id=(group_shift(g, k, 1), t), device_id_type=MESH,
            )
            copy.start()

    for n in range(CHUNKS):
        span = chunk(n)
        rows_n = dot(pick, table[:, span])
        picked[:, :, span] = rows_n.astype(BF16).reshape(GROUPS, 8, span.size)
        if n < AHEAD:
            ask(n)
        arrived[0, :, span] = picked[0, :, span]

    up = ((z + 1) % SIDE) * 2 + c
    down = ((z + SIDE - 1) % SIDE) * 2 + c
    far = ((z + 2) % SIDE) * 2 + c
    twin = z * 2 + 1 - c
    def send(n, number, block, side, target):
        place = tokens[n].at[block]
        if side is not None:
            place = place.at[pl.ds(side * 2 * PAIRS, 2 * PAIRS)]
        copy = pltpu.make_async_remote_copy(
            src_ref=place, dst_ref=place,
            send_sem=ag_s.at[n], recv_sem=ag_r.at[n, number],
            device_id=(g, target), device_id_type=MESH,
        )
        copy.start()

    factor = []

    def own(n):
        wait_bytes(arrived.at[rest, :, chunk(n)], row_r.at[n])
        if n + AHEAD < CHUNKS:
            ask(n + AHEAD)
        piece = PIECES[n]
        if n == 0:
            led = dot(pack, arrived[:, :, pl.ds(0, LEAD)].reshape(SLOTS, LEAD))
            led = led[: 2 * PAIRS]
            factor.append(led[:, 0:1] + led[:, 1:2] + led[:, 2:3])
        got = dot(pack, arrived[:, :, pl.ds(LEAD + STARTS[n], piece)].reshape(SLOTS, piece))
        for h in range(2):
            one = got[h * 2 * PAIRS : (h + 1) * 2 * PAIRS]
            cols = pl.ds(h * half + STARTS[n], piece)
            tokens[n][t, pl.ds(h * 2 * PAIRS, 2 * PAIRS), :] = (
                one * factor[0] * gain_ref[:, cols]
            ).astype(BF16)
            resid[:, cols] = (one[:PAIRS] + one[PAIRS:]) * (1.0 / 16.0)
        for number, target in ((0, up), (1, down), (3, twin)):
            send(n, number, t, None, target)

    def forward_near(n):
        wait_bytes(tokens[n].at[down], ag_r.at[n, 0])
        send(n, 2, down, 0, up)
        send(n, 3, down, None, twin)
        wait_bytes(tokens[n].at[up], ag_r.at[n, 1])
        send(n, 2, up, 1, down)
        send(n, 3, up, None, twin)

    def forward_far(n):
        wait_bytes(tokens[n].at[far], ag_r.at[n, 2])
        send(n, 3, far, None, twin)

    def project(n):
        wait_bytes(tokens[n].at[pl.ds(0, SIDE)], ag_r.at[n, 3])
        depth = 512 if PIECES[n] % 512 == 0 else 256

        def block(h, i):
            cols = pl.ds(pl.multiple_of(i * depth, depth), depth)
            a = tokens[n][:, pl.ds(h * 2 * PAIRS, 2 * PAIRS), cols]
            start = pl.multiple_of(h * half + STARTS[n] + i * depth, 256)
            w = qkv_w[pl.ds(start, depth), :]
            return dot(a.reshape(2 * TENSORS * PAIRS, depth), w)

        if n == 0:
            acc[...] = block(0, 0)
        for h in range(2):

            @pl.loop(1 if n + h == 0 else 0, PIECES[n] // depth)
            def _(i):
                acc[...] += block(h, i)

    steps = (
        (own, 0), (own, 1), (forward_near, 0), (own, 2),
        (forward_near, 1), (own, 3), (forward_far, 0), (forward_near, 2),
        (project, 0), (forward_far, 1), (forward_near, 3), (forward_far, 2),
        (project, 1), (forward_far, 3), (project, 2), (project, 3),
    )
    for step, n in steps:
        if step is project and n == 0:
            for copy in loads[10:13]:
                copy.wait()
        step(n)

    count = 2 * TENSORS * PAIRS

    def column(at):
        return acc[:, pl.ds(at * HEAD_DIM, HEAD_DIM)]

    def unit(rows_):
        return rows_ * lax.rsqrt(jnp.mean(rows_ * rows_, axis=-1, keepdims=True) + 1e-06)

    heads = q_cols // HEAD_DIM
    block = 8
    rows_b = count // 2

    def blocks(values):
        tiles = values.reshape(rows_b // block, 2, block, HEAD_DIM)
        return [tiles[:, n].reshape(rows_b, HEAD_DIM) for n in range(2)]

    keys_b = blocks(unit(column(heads)))
    values_b = blocks(column(heads + 1))
    mask = (iota((rows_b, rows_b), 0) & 7) == (iota((rows_b, rows_b), 1) & 7)
    pool = jnp.where(
        iota((block, rows_b), 0) == (iota((block, rows_b), 1) & 7), 1.0, 0.0
    ).astype(BF16)
    pooled = []
    for head in range(heads):
        halves = []
        for n, query in enumerate(blocks(unit(column(head)))):
            scores = lax.dot_general(
                query.astype(BF16), keys_b[n].astype(BF16), (((1,), (1,)), ((), ())),
                preferred_element_type=F32,
            ) * (SCORE_SCALE / HEAD_DIM)
            expo = jnp.where(mask, jnp.exp(scores), 0.0)
            weights = (expo * (1.0 / jnp.sum(expo, axis=-1, keepdims=True))).astype(BF16)
            context = dot(weights, values_b[n].astype(BF16)).astype(BF16)
            halves.append(dot(pool, context) * (1.0 / 16.0))
        pooled.append(jnp.concatenate(halves, axis=0))
    pooled = jnp.concatenate(pooled, axis=1)
    high = pooled.astype(BF16)
    low = (pooled - high.astype(F32)).astype(BF16)
    both = jnp.concatenate([high, low], axis=0)

    loads[13].wait()
    for j in (4, 5, 2, 3, 6, 7, 1, 0):
        target = ((z + j // 2) % SIDE) * 2 + (c + j % 2) % 2
        cols = pl.ds(pl.multiple_of(target * share, share), share)
        got = dot(both, out_w[:, cols])
        mine = got[:PAIRS] + got[PAIRS:] + resid[:, cols]
        if j > 0:
            part[j] = mine.astype(BF16)
            copy = pltpu.make_async_remote_copy(
                src_ref=part.at[j], dst_ref=parts_in.at[j],
                send_sem=rs_s, recv_sem=rs_r,
                device_id=(g, target), device_id_type=MESH,
            )
            copy.start()
    others = pl.ds(1, TENSORS - 1)
    wait_bytes(parts_in.at[others], rs_r)
    total = mine
    for j in range(1, TENSORS):
        total = total + parts_in[j].astype(F32)
    live = iota((PAIRS, share), 0) < count_ref[...]
    total = jnp.where(live, total, 0.0)

    stacked = jnp.concatenate([total[:, : share // 2], total[:, share // 2 :]], axis=0)
    got = dot(spread, stacked.astype(BF16))
    fin_out[...] = got.astype(BF16).reshape(GROUPS, 8, share // 2)
    for k in ORDER:
        copy = pltpu.make_async_remote_copy(
            src_ref=fin_out.at[k], dst_ref=fin_in.at[k],
            send_sem=fin_s, recv_sem=fin_r,
            device_id=(group_shift(g, k, -1), t), device_id_type=MESH,
        )
        copy.start()
    load(fin_out.at[0], fin_in.at[0])
    wait_bytes(outbox.at[rest], idx_s)
    wait_bytes(picked.at[rest], row_s)
    for n in range(CHUNKS):
        wait_bytes(tokens[n].at[pl.ds(0, TENSORS - 1)], ag_s.at[n])
    wait_bytes(part.at[others], rs_s)
    for copy in loads[14:]:
        copy.wait()
    wait_bytes(fin_out.at[rest], fin_s)
    wait_bytes(fin_in.at[rest], fin_r)


def owner_sums(wanted_ref, came_ref, lout_ref, rout_ref):
    pick = pick_matrix(wanted_ref[...].reshape(SLOTS, 128))
    span = came_ref.shape[2]
    got = lax.dot_general(
        pick, came_ref[...].reshape(SLOTS, span), (((0,), (0,)), ((), ())),
        preferred_element_type=F32,
    )
    for h in range(2):
        for side, out in enumerate((lout_ref, rout_ref)):
            at = (h * 2 + side) * ROWS
            out[:, pl.ds(h * span, span)] = got[at : at + ROWS]


def on_device(
    left_table, right_table, left_owner, left_row, right_owner, right_row, pair_count,
    norm_gain, query_weight, key_weight, value_weight, output_weight,
):
    width = left_table.shape[2]
    half = width // 2
    share = width // TENSORS
    qkv = query_weight.shape[1] + 2 * key_weight.shape[1]
    vmem = pl.BlockSpec(memory_space=pltpu.VMEM)
    hbm = pl.BlockSpec(memory_space=pl.ANY)
    dma = pltpu.SemaphoreType.DMA
    wanted, came = pl.pallas_call(
        kernel,
        out_shape=(
            jax.ShapeDtypeStruct((GROUPS, 8, 128), F32),
            jax.ShapeDtypeStruct((GROUPS, 8, share // 2), BF16),
        ),
        in_specs=[hbm] * 12,
        out_specs=(hbm, hbm),
        scratch_shapes=[
            pltpu.VMEM((1, PAIRS), jnp.int32),
            pltpu.VMEM((1, PAIRS), jnp.int32),
            pltpu.VMEM((1, PAIRS), jnp.int32),
            pltpu.VMEM((1, PAIRS), jnp.int32),
            pltpu.VMEM((1, 1), jnp.int32),
            pltpu.VMEM((1, width), F32),
            pltpu.VMEM((GROUPS, 8, 128), F32),
            pltpu.VMEM((4 * ROWS, LEAD + half), BF16),
            pltpu.VMEM((width, qkv), BF16),
            pltpu.VMEM(output_weight.shape, BF16),
            pltpu.VMEM((GROUPS, 8, 128), F32),
            pltpu.VMEM((GROUPS, 8, LEAD + half), BF16),
            pltpu.VMEM((GROUPS, 8, LEAD + half), BF16),
            pltpu.VMEM((PAIRS, width), F32),
            pltpu.VMEM((2 * TENSORS * PAIRS, qkv), F32),
            pltpu.VMEM((TENSORS, PAIRS, share), BF16),
            pltpu.VMEM((TENSORS, PAIRS, share), BF16),
            pltpu.VMEM((GROUPS, 8, share // 2), BF16),
            dma((16,)),
            dma, dma,
            dma, dma((CHUNKS,)),
            dma((CHUNKS,)), dma((CHUNKS, SIDE)),
            dma, dma,
            dma, dma,
        ]
        + [pltpu.VMEM((TENSORS, 4 * PAIRS, piece), BF16) for piece in PIECES],
        compiler_params=pltpu.CompilerParams(
            collective_id=0, has_side_effects=True, vmem_limit_bytes=56 * 1024 * 1024
        ),
    )(
        left_owner.reshape(1, PAIRS), left_row.reshape(1, PAIRS),
        right_owner.reshape(1, PAIRS), right_row.reshape(1, PAIRS),
        pair_count.reshape(1, 1), norm_gain.reshape(1, width),
        left_table.reshape(ROWS, width), right_table.reshape(ROWS, width),
        query_weight, key_weight, value_weight, output_weight,
    )
    out = jax.ShapeDtypeStruct((ROWS, share), F32)
    return pl.pallas_call(
        owner_sums, out_shape=(out, out), in_specs=[vmem, vmem], out_specs=(vmem, vmem)
    )(wanted, came)


def solution(mesh):
    return jax.shard_map(
        on_device,
        mesh=mesh,
        in_specs=(
            P("group", "tensor", None), P("group", "tensor", None),
            P("group", None), P("group"), P("group", None), P("group"), P("group"), P(),
            P(None, "tensor"), P(None, "tensor"), P(None, "tensor"), P("tensor", None),
        ),
        out_specs=(P("group", "tensor"), P("group", "tensor")),
        check_vma=False,
    )
```
